256 devices in a mesh: face: 32 (over z, y_lo, core), depth: 8 (over y_hi, x).
Axes of the slice: x: 4, y: 4 (y_hi: 2, y_lo: 2; y = y_hi * 2 + y_lo), z: 8, core: 2. Of those that a mesh axis runs over, the one named last changes fastest.
Arguments:
- thermal_field: float32 [2, 32, 8, 2048], P(None, 'face', 'depth'), may hold values from -6 to 6
- lumped_storage: float32 [2, 32, 8, 2048], P(None, 'face', 'depth'), may hold values from 1 to 4
- simplex_vertices: int32 [2, 32, 8, 4, 8192], P(None, 'face', 'depth'), may hold values from 0 to 2047
- stiffness_entries: float32 [2, 32, 8, 10, 8192], P(None, 'face', 'depth'), may hold values from -0.3 to 2, as said below
- interface_vertices: int32 [2, 32, 8, 2, 256], P(None, 'face', 'depth'), may hold values from 0 to 2047, as said below
- touching_triangle_vertices: int32 [2, 32, 3, 1024], P(None, 'face'), may hold values from 0 to 2047
- partner_lookup: int32 [32, 1024], replicated, may hold values from 0 to 32767, as said below
- engaged_flags: int32 [32, 1024], P('face'), may hold values 0 or 1
- rotor_gap_quantities: float32 [3, 32, 1024], P(None, 'face'), may hold values from -6 to 6
- lining_orthogonal_motion: float32 [32, 1024], P('face'), may hold values from -6 to 6
- touching_transfer_factor: float32 [32, 1024], P('face'), may hold values from 2 to 16
Outputs:
- advanced_thermal_field: float32 [2, 32, 8, 2048], P(None, 'face', 'depth')
- pressure: float32 [32, 1024], P('face')
The draws below stay inside these ranges and needn't reach their ends.
Inputs may be any that keep to these rules, and one draw needn't show every extreme that they name: `stiffness_entries`: diagonal entries (the first four components) lie in [1, 2], off-diagonal ones in [-0.3, -0.05]. `interface_vertices`: the two lists of one body on one device name 512 different nodes. Position i of a block's upper list and position i of the lower list of the block above are copies of one node. `partner_lookup`: A disc face may meet a pad face of any patch; several disc faces may meet one pad face.
All inputs are finite; a program needn't handle non-finite values. No bound on the sum of `engaged_flags` on one device may be relied on, other than what follows from the above.
Results may differ from the reference program's by a relative error of at most 0.00002.
Values sent between devices are 32-bit elements; how exact they have to be, the bound alone decides.
No kernel may reach another device: no remote copies, remote signals or barrier semaphores. Data moves between devices by JAX's collectives and lax.ppermute only.
A program may use at most 64 MiB of HBM per device.

```python
import math
import jax
import jax.numpy as jnp
from jax import lax

TET_DEV = 8192
CF = 1024
MESH_POINTS_LOCAL = 2048
IFACE = 256
BOUNDARY_TILES = 32
LAYER_TIERS = 8


def draw_stiffness_entries(key, part):
    array_shape = (2, BOUNDARY_TILES, LAYER_TIERS, 10, TET_DEV)
    base = jax.random.uniform(key, array_shape, jnp.float32)
    component = lax.broadcasted_iota(jnp.int32, array_shape, 3)
    return jnp.where(component < 4, 1.0 + base, -0.05 - 0.25 * base)


def draw_interface_vertices(key, part):
    total = 2 * BOUNDARY_TILES * LAYER_TIERS
    keys = jax.random.split(jax.random.fold_in(key, 17), total)
    orders = jax.vmap(lambda single: jax.random.permutation(single, MESH_POINTS_LOCAL))(keys)
    picked = orders[:, :2 * IFACE].astype(jnp.int32)
    return picked.reshape(2, BOUNDARY_TILES, LAYER_TIERS, 2, IFACE)


def draw_partner_lookup(key, part):
    patch_key, face_key = jax.random.split(jax.random.fold_in(key, 29))
    grid_shape = (BOUNDARY_TILES, CF)
    own_patch = lax.broadcasted_iota(jnp.int32, grid_shape, 0)
    slot = lax.broadcasted_iota(jnp.int32, grid_shape, 1)
    far_patch = jax.random.randint(patch_key, grid_shape, 0, BOUNDARY_TILES, jnp.int32)
    within = jax.random.randint(face_key, grid_shape, 0, CF, jnp.int32)
    far_patch = jnp.where(slot == 0, jnp.mod(own_patch + BOUNDARY_TILES // 2, BOUNDARY_TILES), far_patch)
    within = jnp.where(slot == 0, CF - 1, within)
    far_patch = jnp.where(slot == 1, jnp.mod(own_patch + 1, BOUNDARY_TILES), far_patch)
    within = jnp.where(slot == 1, 0, within)
    return (far_patch * CF + within).astype(jnp.int32)


def touch_ends(array, own_key, low, top_value):
    extent = array.shape
    spot = [jax.random.randint(jax.random.fold_in(own_key, axis), (), 0, extent[axis]) for axis in range(len(extent))]
    array = array.at[tuple(spot)].set(low)
    longest = extent.index(max(extent))
    spot[longest] = (spot[longest] + 1) % extent[longest]
    return array.at[tuple(spot)].set(top_value)


def levels(key, extent, cuts, low, largest):
    def one(axis_at, blocks):
        draws = jax.random.uniform(jax.random.fold_in(jax.random.fold_in(key, 6), axis_at), (blocks,), jnp.float32, low / len(cuts), largest / len(cuts))
        return jnp.repeat(jnp.exp(draws), extent[axis_at] // blocks).reshape((-1,) + (1,) * (len(extent) - axis_at - 1))

    factor_of = one(*cuts[0])
    for cut in cuts[1:]:
        factor_of = factor_of * one(*cut)
    return factor_of


def gaussian(own_key, extent, width, limit, cuts=(), kind=jnp.bfloat16):
    factor_of = levels(own_key, extent, cuts, -0.22, 0.18) if cuts else 1.0
    values = jax.random.normal(own_key, extent, jnp.float32) * width * factor_of
    return jnp.minimum(jnp.maximum(values, -limit), limit).astype(kind)


def setup_inputs(seed: int = 0) -> dict:
    seeds = jax.random.split(jax.random.key(seed), 12)
    thermal_field = gaussian(seeds[0], (2, BOUNDARY_TILES, LAYER_TIERS, MESH_POINTS_LOCAL), 1.0, 6.0, ((1, 32), (2, 8)), jnp.float32)
    lumped_storage = jnp.clip(jnp.exp(math.log(4.0) - 1.3862944 * jax.random.uniform(seeds[1], (2, BOUNDARY_TILES, LAYER_TIERS, MESH_POINTS_LOCAL), jnp.float32) ** levels(seeds[1], (2, BOUNDARY_TILES, LAYER_TIERS, MESH_POINTS_LOCAL), ((1, 32), (2, 8)), -0.2, 0.2)), 1.0, 4.0)
    simplex_vertices = touch_ends(jax.random.randint(seeds[2], (2, BOUNDARY_TILES, LAYER_TIERS, 4, TET_DEV), 0, MESH_POINTS_LOCAL), jax.random.fold_in(seeds[2], 1), 0, MESH_POINTS_LOCAL - 1).astype(jnp.int32)
    stiffness_entries = draw_stiffness_entries(jax.random.fold_in(seeds[11], 71), 0)
    interface_vertices = draw_interface_vertices(jax.random.fold_in(seeds[11], 71), 0)
    touching_triangle_vertices = touch_ends(jax.random.randint(seeds[5], (2, BOUNDARY_TILES, 3, CF), 0, MESH_POINTS_LOCAL), jax.random.fold_in(seeds[5], 1), 0, MESH_POINTS_LOCAL - 1).astype(jnp.int32)
    partner_lookup = draw_partner_lookup(jax.random.fold_in(seeds[11], 71), 0)
    engaged_flags = touch_ends((jax.random.randint(seeds[7], (BOUNDARY_TILES, CF), 0, 4) < 3).astype(jnp.int32), jax.random.fold_in(seeds[7], 1), 0, 1)
    rotor_gap_quantities = gaussian(seeds[8], (3, BOUNDARY_TILES, CF), 1.0, 6.0, ((1, 32),), jnp.float32)
    lining_orthogonal_motion = gaussian(seeds[9], (BOUNDARY_TILES, CF), 1.0, 6.0, ((0, 32),), jnp.float32)
    touching_transfer_factor = jnp.clip(jnp.exp(math.log(16.0) - 2.0794415 * jax.random.uniform(seeds[10], (BOUNDARY_TILES, CF), jnp.float32) ** levels(seeds[10], (BOUNDARY_TILES, CF), ((0, 32),), -0.2, 0.2)), 2.0, 16.0)
    return {"thermal_field": thermal_field, "lumped_storage": lumped_storage, "simplex_vertices": simplex_vertices, "stiffness_entries": stiffness_entries, "interface_vertices": interface_vertices, "touching_triangle_vertices": touching_triangle_vertices, "partner_lookup": partner_lookup, "engaged_flags": engaged_flags, "rotor_gap_quantities": rotor_gap_quantities, "lining_orthogonal_motion": lining_orthogonal_motion, "touching_transfer_factor": touching_transfer_factor}


increment_factor = 0.05
nitsche = 1.0
film_floor = 0.25


def element_residual(values, corners, entries):
    picked = values[corners]
    row_one = entries[0] * picked[0] + entries[4] * picked[1] + entries[5] * picked[2] + entries[6] * picked[3]
    row_two = entries[4] * picked[0] + entries[1] * picked[1] + entries[7] * picked[2] + entries[8] * picked[3]
    row_three = entries[5] * picked[0] + entries[7] * picked[1] + entries[2] * picked[2] + entries[9] * picked[3]
    row_four = entries[6] * picked[0] + entries[8] * picked[1] + entries[9] * picked[2] + entries[3] * picked[3]
    stacked = -jnp.stack([row_one, row_two, row_three, row_four])
    return jax.ops.segment_sum(stacked.reshape(-1), corners.reshape(-1), num_segments=values.shape[0])


def touching_triangle_values(values, corners):
    picked = values[corners]
    return (picked[0] + picked[1] + picked[2]) / 3.0


def spread_faces(face_rates, corners, solid_vertex_total):
    shares = jnp.broadcast_to(face_rates / 3.0, corners.shape)
    return jax.ops.segment_sum(shares.reshape(-1), corners.reshape(-1), num_segments=solid_vertex_total)


def set_rims(values, low_at, up_at, low_set, up_set):
    return values.at[low_at].set(low_set).at[up_at].set(up_set)


def reference(thermal_field, lumped_storage, simplex_vertices, stiffness_entries, interface_vertices, touching_triangle_vertices, partner_lookup, engaged_flags, rotor_gap_quantities, lining_orthogonal_motion, touching_transfer_factor):
    solid_vertex_total = thermal_field.shape[-1]
    simplex_total = simplex_vertices.shape[-1]
    cell_share = lax.map(lambda blocks: element_residual(blocks[0], blocks[1], blocks[2]),
                           (thermal_field.reshape(-1, solid_vertex_total), simplex_vertices.reshape(-1, 4, simplex_total), stiffness_entries.reshape(-1, 10, simplex_total)))
    thermal_imbalance = cell_share.reshape(thermal_field.shape)
    boundary_restrictions = jax.vmap(jax.vmap(touching_triangle_values))(thermal_field[:, :, 0, :], touching_triangle_vertices)
    flat_match = partner_lookup.reshape(-1)
    active_mask = engaged_flags.astype(jnp.float32)
    pad_normals = lining_orthogonal_motion.reshape(-1)[flat_match].reshape(partner_lookup.shape)
    pad_traces = boundary_restrictions[1].reshape(-1)[flat_match].reshape(partner_lookup.shape)
    pressure = active_mask * jnp.maximum(rotor_gap_quantities[2] + nitsche * (rotor_gap_quantities[0] - pad_normals - rotor_gap_quantities[1]), 0.0)
    disc_rate = active_mask * touching_transfer_factor * (film_floor + pressure) * (pad_traces - boundary_restrictions[0])
    pad_rate = -jax.ops.segment_sum(disc_rate.reshape(-1), flat_match, num_segments=flat_match.shape[0]).reshape(partner_lookup.shape)
    face_rates = jnp.stack([disc_rate, pad_rate])
    nodal = jax.vmap(jax.vmap(lambda rates_row, corners: spread_faces(rates_row, corners, solid_vertex_total)))(face_rates, touching_triangle_vertices)
    thermal_imbalance = thermal_imbalance.at[:, :, 0, :].add(nodal)
    lower = interface_vertices[:, :, :, 0, :]
    upper = interface_vertices[:, :, :, 1, :]
    low_values = jnp.take_along_axis(thermal_imbalance, lower, axis=3)
    up_values = jnp.take_along_axis(thermal_imbalance, upper, axis=3)
    zeros_row = jnp.zeros_like(low_values[:, :, :1])
    from_below = jnp.concatenate([zeros_row, up_values[:, :, :-1]], axis=2)
    from_above = jnp.concatenate([low_values[:, :, 1:], zeros_row], axis=2)
    low_new = low_values + from_below
    up_new = up_values + from_above
    rim_count = lower.shape[-1]
    gathered_imbalance = jax.vmap(set_rims)(thermal_imbalance.reshape(-1, solid_vertex_total), lower.reshape(-1, rim_count), upper.reshape(-1, rim_count),
                                   low_new.reshape(-1, rim_count), up_new.reshape(-1, rim_count)).reshape(thermal_imbalance.shape)
    advanced_thermal_field = thermal_field + increment_factor * gathered_imbalance / lumped_storage
    return advanced_thermal_field, pressure
```

```python
import jax
import jax.numpy as jnp
from jax import lax
from jax.experimental import pallas as pl
from jax.experimental.pallas import tpu as pltpu
from jax.sharding import PartitionSpec as P

increment_factor = 0.05
nitsche = 1.0
film_floor = 0.25

LANES = 128
ROWS = 8
LOW = 64


def lane_lookup(row_of, indices, row_total):
    lane = indices & (LANES - 1)
    row = indices >> 7
    level = [
        jnp.take_along_axis(row_of(r), lane, axis=1, mode="promise_in_bounds")
        for r in range(row_total)
    ]
    bit = 0
    while len(level) > 1:
        odd = ((row >> bit) & 1) == 1
        level = [jnp.where(odd, level[k + 1], level[k]) for k in range(0, len(level), 2)]
        bit += 1
    return level[0]


def wide(ref, row, *lead):
    return ref[(*lead, pl.ds(row, ROWS, stride=0), slice(None))]


def split(values):
    coarse = values.astype(jnp.bfloat16).astype(jnp.float32)
    fine = (values - coarse).astype(jnp.bfloat16).astype(jnp.float32)
    return coarse, fine


def high_keys(high_total):
    half = high_total // 2
    keys = []
    for k in range(high_total // ROWS):
        place = lax.broadcasted_iota(jnp.int32, (ROWS, LANES), 0) + k * ROWS
        keys.append((place % half) * 2 + place // half)
    return keys


def low_keys():
    return [lax.broadcasted_iota(jnp.int32, (ROWS, LANES), 0) + k * ROWS for k in range(LOW // ROWS)]


def scatter_operands(index, coarse, fine, highs, lows):
    high = index >> 6
    low = index & (LOW - 1)
    zero = jnp.zeros((ROWS, LANES), jnp.float32)
    hit = [high == key for key in highs]
    values = [jnp.where(h, coarse, zero) for h in hit] + [jnp.where(h, fine, zero) for h in hit]
    one_hot = [jnp.where(low == key, 1.0, 0.0) for key in lows]
    return (
        jnp.concatenate(values, axis=0).astype(jnp.bfloat16),
        jnp.concatenate(one_hot, axis=0).astype(jnp.bfloat16),
    )


def contract(slices):
    values = jnp.concatenate([s[0] for s in slices], axis=1)
    one_hot = jnp.concatenate([s[1] for s in slices], axis=1)
    return lax.dot_general(
        values, one_hot, (((1,), (1,)), ((), ())), preferred_element_type=jnp.float32
    )


def store_nodal(ref, lead, total, scale=None):
    high_total = total.shape[0] // 2
    both = total[:high_total] + total[high_total:]
    if scale is not None:
        both = both * scale
    half = high_total // 2
    ref[(*lead, slice(0, half), slice(0, LOW))] = both[:half]
    ref[(*lead, slice(0, half), slice(LOW, LANES))] = both[half:]


def vmem_specs(count):
    return [pl.BlockSpec(memory_space=pltpu.VMEM) for _ in range(count)]


def packet_kernel(field, corners, motion, engaged, gaps, factor, out):
    for body in range(2):
        picked = [
            lane_lookup(lambda r: wide(field, r, body), corners[body, c], 16) for c in range(3)
        ]
        out[1 + body if body == 0 else 1] = (picked[0] + picked[1] + picked[2]) / 3.0
        if body == 0:
            out[2] = out[1]
    out[0] = motion[...]
    out[3] = engaged[...].astype(jnp.float32) * factor[...]
    out[4] = gaps[2] + nitsche * (gaps[0] - gaps[1])


def element_kernel(field, vertices, entries, rims, out, rim_out, coarse_at, fine_at):
    highs = high_keys(32)
    lows = low_keys()
    chunks = vertices.shape[1] // (4 * ROWS)
    for body in range(2):

        def chunk(j, total):
            corner = [vertices[body, pl.ds(32 * j + c, ROWS, stride=4), :] for c in range(4)]
            picked = [lane_lookup(lambda r: wide(field, r, body), i, 16) for i in corner]
            k = [entries[body, e, pl.ds(pl.multiple_of(ROWS * j, ROWS), ROWS), :] for e in range(10)]
            order = ((0, 4, 5, 6), (4, 1, 7, 8), (5, 7, 2, 9), (6, 8, 9, 3))
            for c in range(4):
                o = order[c]
                row = (
                    k[o[0]] * picked[0]
                    + k[o[1]] * picked[1]
                    + k[o[2]] * picked[2]
                    + k[o[3]] * picked[3]
                )
                coarse, fine = split(row)
                coarse_at[c] = coarse
                fine_at[c] = fine
            for c in range(4):
                slices = [
                    scatter_operands(
                        wide(vertices, 32 * j + 4 * s + c, body),
                        wide(coarse_at, s, c),
                        wide(fine_at, s, c),
                        highs,
                        lows,
                    )
                    for s in range(ROWS)
                ]
                total = total + contract(slices)
            return total

        total = lax.fori_loop(0, chunks, chunk, jnp.zeros((64, LOW), jnp.float32))
        store_nodal(out, (body,), total, -1.0)
    rim_out[...] = rim_lookup(out, rims)


def rim_lookup(nodal, rims):
    index = rims[...]
    first = lane_lookup(lambda r: wide(nodal, r, 0), index, 16)
    second = lane_lookup(lambda r: wide(nodal, r, 1), index, 16)
    place = lax.broadcasted_iota(jnp.int32, (ROWS, LANES), 0)
    return jnp.where(place < 4, first, second)


def contact_kernel(
    where, packets, lookup, gaps, engaged, factor, corners, rims, pressure_out, nodal, rim_out, pads, coarse_at, fine_at
):
    face = where[0]
    surface = (where[1] == 0).astype(jnp.float32)
    own = lookup[face]

    def place_of(patch):
        away = patch ^ face
        return (
            ((away & 1) << 4) | ((away & 2) << 2) | (away & 4) | ((away & 8) >> 2) | ((away & 16) >> 4)
        )

    spot = (place_of(own >> 10) << 10) | (own & 1023)

    def one_packet(p, carry):
        normal, trace = carry
        mine = (spot >> 10) == p
        local = spot & 1023
        normal = jnp.where(mine, lane_lookup(lambda r: wide(packets, r, p, 0), local, 8), normal)
        trace = jnp.where(mine, lane_lookup(lambda r: wide(packets, r, p, 1), local, 8), trace)
        return normal, trace

    zero = jnp.zeros((ROWS, LANES), jnp.float32)
    pad_normal, pad_trace = lax.fori_loop(0, 32, one_packet, (zero, zero))
    active = engaged[...].astype(jnp.float32)
    pressure = active * jnp.maximum(gaps[2] + nitsche * (gaps[0] - pad_normal - gaps[1]), 0.0)
    pressure_out[...] = pressure
    disc_rate = (active * factor[...]) * (film_floor + pressure) * (pad_trace - packets[0, 2])

    highs = high_keys(16)
    lows = low_keys()

    def one_source(p, total):
        source = face ^ place_of(face ^ p)
        index = lookup[source]
        local = index & 1023
        normal = lane_lookup(lambda r: wide(packets, r, 0, 0), local, 8)
        trace = lane_lookup(lambda r: wide(packets, r, 0, 1), local, 8)
        rate = (
            packets[p, 3]
            * (film_floor + jnp.maximum(packets[p, 4] - nitsche * normal, 0.0))
            * (trace - packets[p, 2])
        )
        coarse, fine = split(jnp.where((index >> 10) == face, rate, 0.0))
        coarse_at[0] = coarse
        fine_at[0] = fine
        slices = [
            scatter_operands(
                wide(lookup, s, source) & 1023, wide(coarse_at, s, 0), wide(fine_at, s, 0), highs, lows
            )
            for s in range(ROWS)
        ]
        return total + contract(slices)

    total = lax.fori_loop(0, 32, one_source, jnp.zeros((32, LOW), jnp.float32))
    store_nodal(pads, (), total, -1.0)

    highs = high_keys(32)
    for body in range(2):
        rate = disc_rate if body == 0 else pads[...]
        coarse, fine = split(rate / 3.0 * surface)
        coarse_at[body] = coarse
        fine_at[body] = fine
        total = jnp.zeros((64, LOW), jnp.float32)
        for c in range(3):
            slices = [
                scatter_operands(
                    wide(corners, s, body, c), wide(coarse_at, s, body), wide(fine_at, s, body), highs, lows
                )
                for s in range(ROWS)
            ]
            total = total + contract(slices)
        store_nodal(nodal, (body,), total)
    rim_out[...] = rim_lookup(nodal, rims)


def advance_kernel(field, storage, element, contact, rims, from_below, from_above, contact_below, out, coarse_at, fine_at):
    highs = high_keys(32)
    lows = low_keys()
    place = lax.broadcasted_iota(jnp.int32, (ROWS, LANES), 0)
    below = from_below[...] + contact_below[...]
    values = jnp.where((place & 1) == 0, pltpu.roll(below, 7, 0), pltpu.roll(from_above[...], 1, 0))
    coarse, fine = split(values)
    coarse_at[...] = coarse
    fine_at[...] = fine
    for body in range(2):
        slices = [
            scatter_operands(wide(rims, s), wide(coarse_at, s), wide(fine_at, s), highs, lows)
            for s in range(4 * body, 4 * body + 4)
        ]
        store_nodal(out, (body,), contract(slices))
    total = element[...] + contact[...] + out[...]
    out[...] = field[...] + increment_factor * total / storage[...]


def f32(*shape):
    return jax.ShapeDtypeStruct(shape, jnp.float32)


def call(body, out, arguments, scratch=(), smem=0, name=None, cost=None):
    return pl.pallas_call(
        body,
        out_shape=out,
        in_specs=[pl.BlockSpec(memory_space=pltpu.SMEM)] * smem + vmem_specs(len(arguments) - smem),
        out_specs=jax.tree.map(lambda _: pl.BlockSpec(memory_space=pltpu.VMEM), out),
        scratch_shapes=[pltpu.VMEM(s, jnp.float32) for s in scratch],
        name=name,
        cost_estimate=cost,
    )(*arguments)


def local(
    thermal_field,
    lumped_storage,
    simplex_vertices,
    stiffness_entries,
    interface_vertices,
    touching_triangle_vertices,
    partner_lookup,
    engaged_flags,
    rotor_gap_quantities,
    lining_orthogonal_motion,
    touching_transfer_factor,
):
    field = thermal_field.reshape(2, 16, LANES)
    storage = lumped_storage.reshape(2, 16, LANES)
    vertices = simplex_vertices.reshape(2, 4, 64, LANES).transpose(0, 2, 1, 3).reshape(2, 256, LANES)
    entries = stiffness_entries.reshape(2, 10, 64, LANES)
    rims = interface_vertices.reshape(2, 2, 2, LANES).transpose(0, 2, 1, 3).reshape(8, LANES)
    corners = touching_triangle_vertices.reshape(2, 3, ROWS, LANES)
    lookup = partner_lookup.reshape(32, ROWS, LANES)
    engaged = engaged_flags.reshape(ROWS, LANES)
    gaps = rotor_gap_quantities.reshape(3, ROWS, LANES)
    motion = lining_orthogonal_motion.reshape(ROWS, LANES)
    factor = touching_transfer_factor.reshape(ROWS, LANES)
    where = jnp.stack([lax.axis_index("face"), lax.axis_index("depth")]).astype(jnp.int32)

    packets = call(
        packet_kernel,
        f32(5, ROWS, LANES),
        (field, corners, motion, engaged, gaps, factor),
        name="packet",
    )[None]
    for step in (16, 8, 4, 2, 1):
        other = lax.ppermute(packets, "face", [(i, i ^ step) for i in range(32)])
        packets = jnp.concatenate([packets, other], axis=0)

    element, rim_element = call(
        element_kernel,
        (f32(2, 16, LANES), f32(ROWS, LANES)),
        (field, vertices, entries, rims),
        scratch=((4, ROWS, LANES), (4, ROWS, LANES)),
        name="element",
    )
    up = [(i, i + 1) for i in range(7)]
    down = [(i + 1, i) for i in range(7)]
    from_below = lax.ppermute(rim_element, "depth", up)
    from_above = lax.ppermute(rim_element, "depth", down)

    pressure, contact, rim_contact = call(
        contact_kernel,
        (f32(ROWS, LANES), f32(2, 16, LANES), f32(ROWS, LANES)),
        (where, packets, lookup, gaps, engaged, factor, corners, rims),
        scratch=((ROWS, LANES), (2, ROWS, LANES), (2, ROWS, LANES)),
        smem=1,
        name="contact",
    )
    contact_below = lax.ppermute(rim_contact, "depth", [(0, 1)])
    advanced = call(
        advance_kernel,
        f32(2, 16, LANES),
        (field, storage, element, contact, rims, from_below, from_above, contact_below),
        scratch=((ROWS, LANES), (ROWS, LANES)),
        name="advance",
    )
    return advanced.reshape(thermal_field.shape), pressure.reshape(1, 1024)


def solution(mesh):
    placed = (
        P(None, "face", "depth", None),
        P(None, "face", "depth", None),
        P(None, "face", "depth", None, None),
        P(None, "face", "depth", None, None),
        P(None, "face", "depth", None, None),
        P(None, "face", None, None),
        P(),
        P("face", None),
        P(None, "face", None),
        P("face", None),
        P("face", None),
    )
    return jax.shard_map(
        local,
        mesh=mesh,
        in_specs=placed,
        out_specs=(P(None, "face", "depth", None), P("face", None)),
        check_vma=False,
    )
```

```python
import functools

import jax
import jax.numpy as jnp
from jax import lax
from jax.experimental import pallas as pl
from jax.experimental.pallas import tpu as pltpu
from jax.sharding import PartitionSpec as P

increment_factor = 0.05
nitsche = 1.0
film_floor = 0.25

LANES = 128
ROWS = 8
LOW = 64
AHEAD = (-1, 0, 1, -4, -3, -2, 2, 3)
OWN = 1


def lane_lookup(row_of, indices, row_total):
    lane = indices & (LANES - 1)
    row = indices >> 7
    level = [
        jnp.take_along_axis(row_of(r), lane, axis=1, mode="promise_in_bounds")
        for r in range(row_total)
    ]
    bit = 0
    while len(level) > 1:
        odd = ((row >> bit) & 1) == 1
        level = [jnp.where(odd, level[k + 1], level[k]) for k in range(0, len(level), 2)]
        bit += 1
    return level[0]


def wide(ref, row, *lead):
    return ref[(*lead, pl.ds(row, ROWS, stride=0), slice(None))]


def split(values):
    coarse = values.astype(jnp.bfloat16).astype(jnp.float32)
    fine = (values - coarse).astype(jnp.bfloat16).astype(jnp.float32)
    return coarse, fine


def double(tile):
    return jnp.concatenate([tile, tile], axis=0).astype(jnp.bfloat16)


def keys(total, interleaved=False):
    out = []
    for k in range(total // 16):
        halves = []
        for h in range(2):
            place = lax.broadcasted_iota(jnp.int32, (ROWS, LANES), 0) + (16 * k + ROWS * h)
            if interleaved:
                place = (place % (total // 2)) * 2 + place // (total // 2)
            halves.append(place.astype(jnp.float32))
        out.append(jnp.concatenate(halves, axis=0).astype(jnp.bfloat16))
    return out


def scatter_operands(index, coarse, fine, highs, lows):
    high = double((index >> 6).astype(jnp.float32))
    low = double((index & (LOW - 1)).astype(jnp.float32))
    coarse = double(coarse)
    fine = double(fine)
    zero = jnp.zeros((16, LANES), jnp.bfloat16)
    one = jnp.ones((16, LANES), jnp.bfloat16)
    hit = [high == key for key in highs]
    values = [jnp.where(h, coarse, zero) for h in hit] + [jnp.where(h, fine, zero) for h in hit]
    one_hot = [jnp.where(low == key, one, zero) for key in lows]
    return jnp.concatenate(values, axis=0), jnp.concatenate(one_hot, axis=0)


def contract(slices):
    values = jnp.concatenate([s[0] for s in slices], axis=1)
    one_hot = jnp.concatenate([s[1] for s in slices], axis=1)
    return lax.dot_general(
        values, one_hot, (((1,), (1,)), ((), ())), preferred_element_type=jnp.float32
    )


def store_nodal(ref, lead, total, sign=1.0):
    high_total = total.shape[0] // 2
    both = (total[:high_total] + total[high_total:]) * sign
    half = high_total // 2
    ref[(*lead, slice(0, half), slice(0, LOW))] = both[:half]
    ref[(*lead, slice(0, half), slice(LOW, LANES))] = both[half:]


def packet_kernel(field, corners, motion, engaged, gaps, factor, out):
    trace = []
    for body in range(2):
        picked = [
            lane_lookup(lambda r: wide(field, r, body), corners[body, c], 16) for c in range(3)
        ]
        trace.append((picked[0] + picked[1] + picked[2]) / 3.0)
    out[0, 0] = motion[...]
    out[0, 1] = trace[1]
    out[0, 2] = trace[0]
    out[0, 3] = engaged[...].astype(jnp.float32) * factor[...]
    out[0, 4] = gaps[2] + nitsche * (gaps[0] - gaps[1])


def element_kernel(body, field, vertices, entries, out, coarse_at, fine_at):
    highs = keys(32, True)
    lows = keys(LOW)
    total = jnp.zeros((64, LOW), jnp.float32)
    order = ((0, 4, 5, 6), (4, 1, 7, 8), (5, 7, 2, 9), (6, 8, 9, 3))
    for j in range(8):
        here = slice(ROWS * j, ROWS * (j + 1))
        corner = [vertices[body, pl.ds(32 * j + c, ROWS, stride=4), :] for c in range(4)]
        picked = [lane_lookup(lambda r: wide(field, r, body), i, 16) for i in corner]
        k = [entries[body, e, here, :] for e in range(10)]
        for c in range(4):
            o = order[c]
            row = (
                k[o[0]] * picked[0]
                + k[o[1]] * picked[1]
                + k[o[2]] * picked[2]
                + k[o[3]] * picked[3]
            )
            coarse, fine = split(row)
            coarse_at[c, here] = coarse
            fine_at[c, here] = fine
        slices = [
            scatter_operands(
                wide(vertices, 32 * j + 4 * s + c, body),
                wide(coarse_at, ROWS * j + s, c),
                wide(fine_at, ROWS * j + s, c),
                highs,
                lows,
            )
            for c in range(4)
            for s in range(ROWS)
        ]
        total = total + contract(slices)
    store_nodal(out, (), total, -1.0)


def rim_lookup(first_row, second_row, index):
    first = lane_lookup(first_row, index, 16)
    second = lane_lookup(second_row, index, 16)
    place = lax.broadcasted_iota(jnp.int32, (ROWS, LANES), 0)
    return jnp.where(place < 4, first, second)


def rim_kernel(disc, pad, rims, out):
    out[...] = rim_lookup(lambda r: wide(disc, r), lambda r: wide(pad, r), rims[...])


def source_of(face, place):
    z = (face >> 2) + AHEAD[place % 8]
    near = (face & 3) ^ ((2 if place & 8 else 0) | (1 if place & 16 else 0))
    return ((z & 7) << 2) | near


def packet_work(face, places, packet_of, own, lookup, normal, trace, total, coarse_at, fine_at):
    highs = keys(16, True)
    lows = keys(LOW)
    mine = lookup[face]
    for group in range(0, len(places), 4):
        slices = []
        for n in range(group, group + 4):
            ref, at = packet_of(places[n])
            source = source_of(face, places[n])
            chosen = (mine >> 10) == source
            local = mine & 1023
            normal = jnp.where(chosen, lane_lookup(lambda r: wide(ref, r, at, 0), local, 8), normal)
            trace = jnp.where(chosen, lane_lookup(lambda r: wide(ref, r, at, 1), local, 8), trace)

            index = lookup[source]
            local = index & 1023
            pad_normal = lane_lookup(lambda r: wide(own, r, 0, 0), local, 8)
            pad_trace = lane_lookup(lambda r: wide(own, r, 0, 1), local, 8)
            rate = (
                ref[at, 3]
                * (film_floor + jnp.maximum(ref[at, 4] - nitsche * pad_normal, 0.0))
                * (pad_trace - ref[at, 2])
            )
            coarse, fine = split(jnp.where((index >> 10) == face, rate, 0.0))
            coarse_at[n] = coarse
            fine_at[n] = fine
            slices += [
                scatter_operands(
                    wide(lookup, s, source) & 1023,
                    wide(coarse_at, s, n),
                    wide(fine_at, s, n),
                    highs,
                    lows,
                )
                for s in range(ROWS)
            ]
        total = total + contract(slices)
    return normal, trace, total


def early_kernel(places, own_first, where, *refs):
    packets, lookup, own = refs[0], refs[1], refs[2]
    before, after, scratch = refs[3:-5], refs[-5:-2], refs[-2:]
    if own_first:
        zero = jnp.zeros((ROWS, LANES), jnp.float32)
        start = (zero, zero, jnp.zeros((32, LOW), jnp.float32))
    else:
        start = tuple(b[...] for b in before)
    done = packet_work(
        where[0], places, lambda p: (packets, p - places[0]), own, lookup, *start, *scratch
    )
    for ref, value in zip(after, done):
        ref[...] = value


def contact_kernel(
    places, where, packets, lookup, own, normal, trace, total, gaps, engaged, factor, corners, rims, disc, pad,
    pressure_out, nodal, rim_out, pads, coarse_at, fine_at,
):
    face = where[0]
    surface = (where[1] == 0).astype(jnp.float32)
    pad_normal, pad_trace, total = packet_work(
        face, places, lambda p: (packets, p - places[0]), own, lookup,
        normal[...], trace[...], total[...], coarse_at, fine_at,
    )
    active = engaged[...].astype(jnp.float32)
    pressure = active * jnp.maximum(gaps[2] + nitsche * (gaps[0] - pad_normal - gaps[1]), 0.0)
    pressure_out[...] = pressure
    disc_rate = (active * factor[...]) * (film_floor + pressure) * (pad_trace - own[0, 2])
    store_nodal(pads, (), total, -1.0)

    highs = keys(32, True)
    lows = keys(LOW)
    for body in range(2):
        rate = disc_rate if body == 0 else pads[...]
        coarse, fine = split(rate / 3.0 * surface)
        at = len(places) + body
        coarse_at[at] = coarse
        fine_at[at] = fine
        slices = [
            scatter_operands(
                wide(corners, s, body, c), wide(coarse_at, s, at), wide(fine_at, s, at), highs, lows
            )
            for c in range(3)
            for s in range(ROWS)
        ]
        store_nodal(nodal, (body,), contract(slices))
        nodal[body] = nodal[body] + (disc if body == 0 else pad)[...]
    rim_out[...] = rim_lookup(lambda r: wide(nodal, r, 0), lambda r: wide(nodal, r, 1), rims[...])


def advance_kernel(where, field, storage, nodal, rims, early, late, out, coarse_at, fine_at):
    highs = keys(32, True)
    lows = keys(LOW)
    place = lax.broadcasted_iota(jnp.int32, (ROWS, LANES), 0)
    even = (where[1] & 1) == 0
    above = jnp.where(even, late[...], early[...])
    below = jnp.where(even, early[...], late[...])
    values = jnp.where((place & 1) == 0, pltpu.roll(below, 7, 0), pltpu.roll(above, 1, 0))
    coarse, fine = split(values)
    coarse_at[...] = coarse
    fine_at[...] = fine
    for body in range(2):
        slices = [
            scatter_operands(wide(rims, s), wide(coarse_at, s), wide(fine_at, s), highs, lows)
            for s in range(4 * body, 4 * body + 4)
        ]
        store_nodal(out, (body,), contract(slices))
    total = nodal[...] + out[...]
    out[...] = field[...] + increment_factor * total / storage[...]


def here(*shape):
    return pltpu.VMEM(shape, jnp.float32)


def near(array):
    return pltpu.with_memory_space_constraint(array, pltpu.VMEM)


def call(body, out, arguments, scratch=(), smem=0, name=None, time=1.0):
    return pl.pallas_call(
        body,
        out_shape=out,
        in_specs=[pl.BlockSpec(memory_space=pltpu.SMEM)] * smem
        + [pl.BlockSpec(memory_space=pltpu.VMEM)] * (len(arguments) - smem),
        out_specs=jax.tree.map(lambda _: pl.BlockSpec(memory_space=pltpu.VMEM), out),
        scratch_shapes=[pltpu.VMEM(s, jnp.float32) for s in scratch],
        name=name,
        cost_estimate=pl.CostEstimate(
            flops=0, transcendentals=0, bytes_accessed=int(time * 3.6e6)
        ),
    )(*arguments)


def local(
    thermal_field,
    lumped_storage,
    simplex_vertices,
    stiffness_entries,
    interface_vertices,
    touching_triangle_vertices,
    partner_lookup,
    engaged_flags,
    rotor_gap_quantities,
    lining_orthogonal_motion,
    touching_transfer_factor,
):
    field = thermal_field.reshape(2, 16, LANES)
    storage = lumped_storage.reshape(2, 16, LANES)
    vertices = simplex_vertices.reshape(2, 4, 64, LANES).transpose(0, 2, 1, 3).reshape(2, 256, LANES)
    entries = stiffness_entries.reshape(2, 10, 64, LANES)
    rims = interface_vertices.reshape(2, 2, 2, LANES).transpose(0, 2, 1, 3).reshape(8, LANES)
    corners = touching_triangle_vertices.reshape(2, 3, ROWS, LANES)
    lookup = partner_lookup.reshape(32, ROWS, LANES)
    engaged = engaged_flags.reshape(ROWS, LANES)
    gaps = rotor_gap_quantities.reshape(3, ROWS, LANES)
    motion = lining_orthogonal_motion.reshape(ROWS, LANES)
    factor = touching_transfer_factor.reshape(ROWS, LANES)
    where = jnp.stack([lax.axis_index("face"), lax.axis_index("depth")]).astype(jnp.int32)
    tile = here(ROWS, LANES)

    def along(cells, step):
        return lax.ppermute(cells, "face", [(i, (i + 4 * step) % 32) for i in range(32)])

    def across(cells, bit):
        return lax.ppermute(cells, "face", [(i, i ^ bit) for i in range(32)])

    def element(body, temperatures):
        return call(
            functools.partial(element_kernel, body),
            here(16, LANES),
            (temperatures, vertices, entries),
            scratch=((4, 64, LANES), (4, 64, LANES)),
            name="element",
            time=2.5,
        )

    own = call(
        packet_kernel,
        here(1, 5, ROWS, LANES),
        (field, corners, motion, engaged, gaps, factor),
        name="packet",
    )
    behind = along(own, 1)
    ahead = along(own, -1)
    disc = element(0, field)
    behind, ahead, disc = lax.optimization_barrier((behind, ahead, disc))
    three = jnp.concatenate([behind, own, ahead], axis=0)
    three, again = lax.optimization_barrier((three, field))
    far_behind = along(three, 3)
    far_ahead = along(three[:2], -3)
    pad = element(1, again)
    far_behind, far_ahead, disc, pad = lax.optimization_barrier((far_behind, far_ahead, disc, pad))
    eight = jnp.concatenate([three, far_behind, far_ahead], axis=0)

    other = across(eight, 2)
    rim_element = call(rim_kernel, tile, (near(disc), near(pad), rims), name="rim", time=0.5)
    early = lax.ppermute(rim_element, "depth", [(1, 2), (2, 1), (3, 4), (4, 3), (5, 6), (6, 5)])
    sums = call(
        functools.partial(early_kernel, tuple(range(8)), True),
        (tile, tile, here(32, LOW)),
        (where, near(eight), lookup, near(own)),
        scratch=((8, ROWS, LANES), (8, ROWS, LANES)),
        smem=1,
        name="first_packets",
    )
    other, sums, early = lax.optimization_barrier((other, sums, early))
    sixteen = jnp.concatenate([eight, other], axis=0)
    last = across(sixteen, 1)
    sums = call(
        functools.partial(early_kernel, tuple(range(8, 16)), False),
        (tile, tile, here(32, LOW)),
        (where, near(other), lookup, near(own), *map(near, sums)),
        scratch=((8, ROWS, LANES), (8, ROWS, LANES)),
        smem=1,
        name="second_packets",
    )
    last, sums = lax.optimization_barrier((last, sums))
    pressure, nodal, rim_total = call(
        functools.partial(contact_kernel, tuple(range(16, 32))),
        (tile, here(2, 16, LANES), tile),
        (
            where, near(last), lookup, near(own), *map(near, sums),
            gaps, engaged, factor, corners, rims, near(disc), near(pad),
        ),
        scratch=((ROWS, LANES), (18, ROWS, LANES), (18, ROWS, LANES)),
        smem=1,
        name="contact",
    )
    late = lax.ppermute(rim_total, "depth", [(i, i ^ 1) for i in range(8)])
    advanced = call(
        advance_kernel,
        jax.ShapeDtypeStruct((2, 16, LANES), jnp.float32),
        (where, field, storage, near(nodal), rims, near(early), near(late)),
        scratch=((ROWS, LANES), (ROWS, LANES)),
        smem=1,
        name="advance",
    )
    return advanced.reshape(thermal_field.shape), pressure.reshape(1, 1024)


def solution(mesh):
    placed = (
        P(None, "face", "depth", None),
        P(None, "face", "depth", None),
        P(None, "face", "depth", None, None),
        P(None, "face", "depth", None, None),
        P(None, "face", "depth", None, None),
        P(None, "face", None, None),
        P(),
        P("face", None),
        P(None, "face", None),
        P("face", None),
        P("face", None),
    )
    return jax.shard_map(
        local,
        mesh=mesh,
        in_specs=placed,
        out_specs=(P(None, "face", "depth", None), P("face", None)),
        check_vma=False,
    )
```

```python
import functools

import jax
import jax.numpy as jnp
from jax import lax
from jax.experimental import pallas as pl
from jax.experimental.pallas import tpu as pltpu
from jax.sharding import PartitionSpec as P

increment_factor = 0.05
nitsche = 1.0
film_floor = 0.25

LANES = 128
ROWS = 8
LOW = 64
AHEAD = (-3, 0, 3, -4, -1, 2, -2, 1)


def lane_lookup(row_of, indices, row_total):
    lane = indices & (LANES - 1)
    row = indices >> 7
    level = [
        jnp.take_along_axis(row_of(r), lane, axis=1, mode="promise_in_bounds")
        for r in range(row_total)
    ]
    bit = 0
    while len(level) > 1:
        odd = ((row >> bit) & 1) == 1
        level = [jnp.where(odd, level[k + 1], level[k]) for k in range(0, len(level), 2)]
        bit += 1
    return level[0]


def wide(ref, row, *lead):
    return ref[(*lead, pl.ds(row, ROWS, stride=0), slice(None))]


def split(values):
    coarse = values.astype(jnp.bfloat16).astype(jnp.float32)
    fine = (values - coarse).astype(jnp.bfloat16).astype(jnp.float32)
    return coarse, fine


def double(tile):
    return jnp.concatenate([tile, tile], axis=0).astype(jnp.bfloat16)


def keys(total, interleaved=False):
    out = []
    for k in range(total // 16):
        halves = []
        for h in range(2):
            place = lax.broadcasted_iota(jnp.int32, (ROWS, LANES), 0) + (16 * k + ROWS * h)
            if interleaved:
                place = (place % (total // 2)) * 2 + place // (total // 2)
            halves.append(place.astype(jnp.float32))
        out.append(jnp.concatenate(halves, axis=0).astype(jnp.bfloat16))
    return out


def scatter_operands(index, coarse, fine, highs, lows):
    high = double((index >> 6).astype(jnp.float32))
    low = double((index & (LOW - 1)).astype(jnp.float32))
    coarse = double(coarse)
    fine = double(fine)
    zero = jnp.zeros((16, LANES), jnp.bfloat16)
    one = jnp.ones((16, LANES), jnp.bfloat16)
    hit = [high == key for key in highs]
    values = [jnp.where(h, coarse, zero) for h in hit] + [jnp.where(h, fine, zero) for h in hit]
    one_hot = [jnp.where(low == key, one, zero) for key in lows]
    return jnp.concatenate(values, axis=0), jnp.concatenate(one_hot, axis=0)


def contract(slices):
    values = jnp.concatenate([s[0] for s in slices], axis=1)
    one_hot = jnp.concatenate([s[1] for s in slices], axis=1)
    return lax.dot_general(
        values, one_hot, (((1,), (1,)), ((), ())), preferred_element_type=jnp.float32
    )


def store_nodal(ref, lead, total, sign=1.0):
    high_total = total.shape[0] // 2
    both = (total[:high_total] + total[high_total:]) * sign
    half = high_total // 2
    ref[(*lead, slice(0, half), slice(0, LOW))] = both[:half]
    ref[(*lead, slice(0, half), slice(LOW, LANES))] = both[half:]


def packet_kernel(field, corners, motion, engaged, gaps, factor, out, corners_out):
    trace = []
    for body in range(2):
        picked = [
            lane_lookup(lambda r: wide(field, r, body), corners[body, c], 16) for c in range(3)
        ]
        trace.append((picked[0] + picked[1] + picked[2]) / 3.0)
    out[0, 0] = motion[...]
    out[0, 1] = trace[1]
    out[0, 2] = trace[0]
    out[0, 3] = engaged[...].astype(jnp.float32) * factor[...]
    out[0, 4] = gaps[2] + nitsche * (gaps[0] - gaps[1])
    corners_out[...] = corners[...]


def element_sum(field, vertices, entries, out, coarse_at, fine_at):
    highs = keys(32, True)
    lows = keys(LOW)
    total = jnp.zeros((64, LOW), jnp.float32)
    order = ((0, 4, 5, 6), (4, 1, 7, 8), (5, 7, 2, 9), (6, 8, 9, 3))
    for j in range(8):
        here = slice(ROWS * j, ROWS * (j + 1))
        corner = [vertices[0, pl.ds(32 * j + c, ROWS, stride=4), :] for c in range(4)]
        picked = [lane_lookup(lambda r: wide(field, r, 0), i, 16) for i in corner]
        k = [entries[0, e, here, :] for e in range(10)]
        for c in range(4):
            o = order[c]
            row = (
                k[o[0]] * picked[0]
                + k[o[1]] * picked[1]
                + k[o[2]] * picked[2]
                + k[o[3]] * picked[3]
            )
            coarse, fine = split(row)
            coarse_at[c, here] = coarse
            fine_at[c, here] = fine
        slices = [
            scatter_operands(
                wide(vertices, 32 * j + 4 * s + c, 0),
                wide(coarse_at, ROWS * j + s, c),
                wide(fine_at, ROWS * j + s, c),
                highs,
                lows,
            )
            for c in range(4)
            for s in range(ROWS)
        ]
        total = total + contract(slices)
    store_nodal(out, (), total, -1.0)


def disc_kernel(field, vertices, entries, partners, out, lookup, coarse_at, fine_at):
    for g in range(4):
        for s in range(ROWS):
            lookup[pl.ds(64 * g + s, ROWS, stride=ROWS), :] = partners[
                ROWS * g : ROWS * (g + 1), LANES * s : LANES * (s + 1)
            ]
    element_sum(field, vertices, entries, out, coarse_at, fine_at)


def rim_lookup(first_row, second_row, index):
    first = lane_lookup(first_row, index, 16)
    second = lane_lookup(second_row, index, 16)
    place = lax.broadcasted_iota(jnp.int32, (ROWS, LANES), 0)
    return jnp.where(place < 4, first, second)


def pad_kernel(
    field, vertices, entries, rims, whole, storage, disc,
    out, rim_out, rims_out, slot_out, field_out, storage_out, coarse_at, fine_at,
):
    rims_out[...] = rims[...]
    field_out[...] = whole[...]
    storage_out[...] = storage[...]
    highs = keys(32, True)
    lows = keys(LOW)
    lane = lax.broadcasted_iota(jnp.int32, (ROWS, LANES), 1)
    for body in range(2):
        slices = []
        for s in range(4):
            coarse, fine = split((lane + (LANES * s + 1)).astype(jnp.float32))
            slices.append(scatter_operands(wide(rims, 4 * body + s), coarse, fine, highs, lows))
        store_nodal(slot_out, (body,), contract(slices))
    element_sum(field, vertices, entries, out, coarse_at, fine_at)
    rim_out[...] = rim_lookup(lambda r: wide(disc, r), lambda r: wide(out, r), rims[...])


def source_of(face, place):
    z = (face >> 2) + AHEAD[place % 8]
    near = (face & 3) ^ ((2 if place & 8 else 0) | (1 if place & 16 else 0))
    return ((z & 7) << 2) | near


def packet_work(face, packets, own, lookup, normal, trace, total, coarse_at, fine_at):
    highs = keys(16, True)
    lows = keys(LOW)
    mine = lookup[pl.ds(pl.multiple_of(face * ROWS, ROWS), ROWS), :]
    n = 0
    for ref, first in packets:
        for group in range(0, 8, 4):
            slices = []
            for at in range(group, group + 4):
                source = source_of(face, first + at)
                chosen = (mine >> 10) == source
                local = mine & 1023
                normal = jnp.where(chosen, lane_lookup(lambda r: wide(ref, r, at, 0), local, 8), normal)
                trace = jnp.where(chosen, lane_lookup(lambda r: wide(ref, r, at, 1), local, 8), trace)

                index = lookup[pl.ds(pl.multiple_of(source * ROWS, ROWS), ROWS), :]
                local = index & 1023
                pad_normal = lane_lookup(lambda r: wide(own, r, 0, 0), local, 8)
                pad_trace = lane_lookup(lambda r: wide(own, r, 0, 1), local, 8)
                rate = (
                    ref[at, 3]
                    * (film_floor + jnp.maximum(ref[at, 4] - nitsche * pad_normal, 0.0))
                    * (pad_trace - ref[at, 2])
                )
                coarse, fine = split(jnp.where((index >> 10) == face, rate, 0.0))
                coarse_at[n] = coarse
                fine_at[n] = fine
                slices += [
                    scatter_operands(
                        wide(lookup, source * ROWS + s) & 1023,
                        wide(coarse_at, s, n),
                        wide(fine_at, s, n),
                        highs,
                        lows,
                    )
                    for s in range(ROWS)
                ]
                n += 1
            total = total + contract(slices)
    return normal, trace, total


def first_kernel(eight, twin, lookup, own, normal_out, trace_out, total_out, coarse_at, fine_at):
    zero = jnp.zeros((ROWS, LANES), jnp.float32)
    normal_out[...], trace_out[...], total_out[...] = packet_work(
        lax.axis_index("face"), ((eight, 0), (twin, 16)), own, lookup,
        zero, zero, jnp.zeros((32, LOW), jnp.float32), coarse_at, fine_at,
    )


def second_kernel(
    other, lookup, own, normal, trace, total, normal_out, trace_out, total_out, coarse_at, fine_at
):
    normal_out[...], trace_out[...], total_out[...] = packet_work(
        lax.axis_index("face"), ((other, 8),), own, lookup,
        normal[...], trace[...], total[...], coarse_at, fine_at,
    )


def contact_kernel(
    last, lookup, own, normal, trace, total, corners, rims, disc, pad,
    pressure_out, nodal, rim_out, pads, coarse_at, fine_at,
):
    surface = (lax.axis_index("depth") == 0).astype(jnp.float32)
    pad_normal, pad_trace, total = packet_work(
        lax.axis_index("face"), ((last, 24),), own, lookup,
        normal[...], trace[...], total[...], coarse_at, fine_at,
    )
    weight = own[0, 3]
    pressure = jnp.where(
        weight != 0.0, jnp.maximum(own[0, 4] - nitsche * pad_normal, 0.0), 0.0
    )
    pressure_out[...] = pressure
    disc_rate = weight * (film_floor + pressure) * (pad_trace - own[0, 2])
    store_nodal(pads, (), total, -1.0)

    highs = keys(32, True)
    lows = keys(LOW)
    for body in range(2):
        rate = disc_rate if body == 0 else pads[...]
        coarse, fine = split(rate / 3.0 * surface)
        at = 8 + body
        coarse_at[at] = coarse
        fine_at[at] = fine
        slices = [
            scatter_operands(
                wide(corners, s, body, c), wide(coarse_at, s, at), wide(fine_at, s, at), highs, lows
            )
            for c in range(3)
            for s in range(ROWS)
        ]
        store_nodal(nodal, (body,), contract(slices))
        nodal[body] = nodal[body] + (disc if body == 0 else pad)[...]
    rim_out[...] = rim_lookup(lambda r: wide(nodal, r, 0), lambda r: wide(nodal, r, 1), rims[...])


def advance_kernel(field, storage, nodal, slots, early, late, out, gained):
    place = lax.broadcasted_iota(jnp.int32, (ROWS, LANES), 0)
    even = (lax.axis_index("depth") & 1) == 0
    above = jnp.where(even, late[...], early[...])
    below = jnp.where(even, early[...], late[...])
    gained[...] = jnp.where((place & 1) == 0, pltpu.roll(below, 7, 0), pltpu.roll(above, 1, 0))
    for body in range(2):
        for half in range(2):
            here = slice(ROWS * half, ROWS * (half + 1))
            slot = slots[body, here].astype(jnp.int32)
            found = lane_lookup(
                lambda r: wide(gained, 4 * body + r), jnp.maximum(slot - 1, 0), 4
            )
            total = nodal[body, here] + jnp.where(slot > 0, found, 0.0)
            out[body, here] = field[body, here] + increment_factor * total / storage[body, here]


def here(*shape, dtype=jnp.float32):
    return pltpu.VMEM(shape, dtype)


def near(array):
    return pltpu.with_memory_space_constraint(array, pltpu.VMEM)


def one_body(array, body):
    block = (1,) + array.shape[1:]
    return pl.BlockSpec(block, lambda i: (body,) + (0,) * (len(block) - 1), memory_space=pltpu.VMEM)


def call(body, out, arguments, scratch=(), specs=None, name=None, time=1.0):
    whole = pl.BlockSpec(memory_space=pltpu.VMEM)
    specs = specs or {}
    return pl.pallas_call(
        body,
        out_shape=out,
        in_specs=[specs.get(i, whole) for i in range(len(arguments))],
        out_specs=jax.tree.map(lambda _: whole, out),
        scratch_shapes=[pltpu.VMEM(s, jnp.float32) for s in scratch],
        grid=(1,) if specs else (),
        name=name,
        cost_estimate=pl.CostEstimate(
            flops=0, transcendentals=0, bytes_accessed=int(time * 3.6e6)
        ),
    )(*arguments)


def local(
    thermal_field,
    lumped_storage,
    simplex_vertices,
    stiffness_entries,
    interface_vertices,
    touching_triangle_vertices,
    partner_lookup,
    engaged_flags,
    rotor_gap_quantities,
    lining_orthogonal_motion,
    touching_transfer_factor,
):
    field = thermal_field.reshape(2, 16, LANES)
    storage = lumped_storage.reshape(2, 16, LANES)
    vertices = simplex_vertices.reshape(2, 4, 64, LANES).transpose(0, 2, 1, 3).reshape(2, 256, LANES)
    entries = stiffness_entries.reshape(2, 10, 64, LANES)
    rims = interface_vertices.reshape(2, 2, 2, LANES).transpose(0, 2, 1, 3).reshape(8, LANES)
    corners = touching_triangle_vertices.reshape(2, 3, ROWS, LANES)
    engaged = engaged_flags.reshape(ROWS, LANES)
    gaps = rotor_gap_quantities.reshape(3, ROWS, LANES)
    motion = lining_orthogonal_motion.reshape(ROWS, LANES)
    factor = touching_transfer_factor.reshape(ROWS, LANES)
    tile = here(ROWS, LANES)
    nodes = here(16, LANES)
    sums = (tile, tile, here(32, LOW))

    def along(cells, step):
        return lax.ppermute(cells, "face", [(i, (i + 4 * step) % 32) for i in range(32)])

    def across(cells, bit):
        return lax.ppermute(cells, "face", [(i, i ^ bit) for i in range(32)])

    def of_body(body):
        return {k: one_body(a, body) for k, a in enumerate((field, vertices, entries))}

    parts = ((4, 64, LANES), (4, 64, LANES))
    own, corners = call(
        packet_kernel,
        (here(1, 5, ROWS, LANES), here(2, 3, ROWS, LANES, dtype=jnp.int32)),
        (field, corners, motion, engaged, gaps, factor),
        name="packet",
    )
    behind = along(own, 3)
    ahead = along(own, -3)
    disc, lookup = call(
        disc_kernel,
        (nodes, here(256, LANES, dtype=jnp.int32)),
        (field, vertices, entries, partner_lookup),
        scratch=parts,
        specs=of_body(0),
        name="disc_element",
        time=2.2,
    )
    behind, ahead, disc, lookup = lax.optimization_barrier((behind, ahead, disc, lookup))
    three = jnp.concatenate([behind, own, ahead], axis=0)
    three, again = lax.optimization_barrier((three, field))
    near_behind = along(three, 1)
    near_ahead = along(three[:2], -1)
    pad, rim_element, rims, slots, field_near, storage_near = call(
        pad_kernel,
        (nodes, tile, here(ROWS, LANES, dtype=jnp.int32)) + (here(2, 16, LANES),) * 3,
        (again, vertices, entries, rims, field, storage, near(disc)),
        scratch=parts,
        specs=of_body(1),
        name="pad_element",
        time=2.5,
    )
    near_behind, near_ahead, pad, rim_element = lax.optimization_barrier(
        (near_behind, near_ahead, pad, rim_element)
    )
    eight = jnp.concatenate([three, near_behind, near_ahead], axis=0)

    other = across(eight, 2)
    twin = across(eight, 1)
    early = lax.ppermute(rim_element, "depth", [(1, 2), (2, 1), (3, 4), (4, 3), (5, 6), (6, 5)])
    done = call(
        first_kernel,
        sums,
        (near(eight), near(twin), near(lookup), near(own)),
        scratch=((16, ROWS, LANES), (16, ROWS, LANES)),
        name="first_packets",
        time=1.5,
    )
    other, done, early = lax.optimization_barrier((other, done, early))
    last = across(other, 1)
    done = call(
        second_kernel,
        sums,
        (near(other), near(lookup), near(own), *map(near, done)),
        scratch=((8, ROWS, LANES), (8, ROWS, LANES)),
        name="second_packets",
    )
    last, done = lax.optimization_barrier((last, done))
    pressure, nodal, rim_total = call(
        contact_kernel,
        (tile, here(2, 16, LANES), tile),
        tuple(map(near, (last, lookup, own, *done, corners, rims, disc, pad))),
        scratch=((ROWS, LANES), (10, ROWS, LANES), (10, ROWS, LANES)),
        name="contact",
        time=1.5,
    )
    late = lax.ppermute(rim_total, "depth", [(i, i ^ 1) for i in range(8)])
    advanced = call(
        advance_kernel,
        jax.ShapeDtypeStruct((2, 16, LANES), jnp.float32),
        tuple(map(near, (field_near, storage_near, nodal, slots, early, late))),
        scratch=((ROWS, LANES),),
        name="advance",
    )
    return advanced.reshape(thermal_field.shape), pressure.reshape(1, 1024)


def solution(mesh):
    placed = (
        P(None, "face", "depth", None),
        P(None, "face", "depth", None),
        P(None, "face", "depth", None, None),
        P(None, "face", "depth", None, None),
        P(None, "face", "depth", None, None),
        P(None, "face", None, None),
        P(),
        P("face", None),
        P(None, "face", None),
        P("face", None),
        P("face", None),
    )
    return jax.shard_map(
        local,
        mesh=mesh,
        in_specs=placed,
        out_specs=(P(None, "face", "depth", None), P("face", None)),
        check_vma=False,
    )
```

```python
import functools

import jax
import jax.numpy as jnp
from jax import lax
from jax.experimental import pallas as pl
from jax.experimental.pallas import tpu as pltpu
from jax.sharding import PartitionSpec as P

increment_factor = 0.05
nitsche = 1.0
film_floor = 0.25

LANES = 128
ROWS = 8
LOW = 64
AHEAD = (-1, 0, 1, -4, -3, -2, 2, 3)


def lane_lookup(row_of, indices, row_total):
    lane = indices & (LANES - 1)
    row = indices >> 7
    level = [
        jnp.take_along_axis(row_of(r), lane, axis=1, mode="promise_in_bounds")
        for r in range(row_total)
    ]
    bit = 0
    while len(level) > 1:
        odd = ((row >> bit) & 1) == 1
        level = [jnp.where(odd, level[k + 1], level[k]) for k in range(0, len(level), 2)]
        bit += 1
    return level[0]


def wide(ref, row, *lead):
    return ref[(*lead, pl.ds(row, ROWS, stride=0), slice(None))]


def split(values):
    coarse = values.astype(jnp.bfloat16).astype(jnp.float32)
    fine = (values - coarse).astype(jnp.bfloat16).astype(jnp.float32)
    return coarse, fine


def double(tile):
    return jnp.concatenate([tile, tile], axis=0).astype(jnp.bfloat16)


def keys(total, interleaved=False):
    out = []
    for k in range(total // 16):
        halves = []
        for h in range(2):
            place = lax.broadcasted_iota(jnp.int32, (ROWS, LANES), 0) + (16 * k + ROWS * h)
            if interleaved:
                place = (place % (total // 2)) * 2 + place // (total // 2)
            halves.append(place.astype(jnp.float32))
        out.append(jnp.concatenate(halves, axis=0).astype(jnp.bfloat16))
    return out


def scatter_operands(index, coarse, fine, highs, lows):
    high = double((index >> 6).astype(jnp.float32))
    low = double((index & (LOW - 1)).astype(jnp.float32))
    coarse = double(coarse)
    fine = double(fine)
    zero = jnp.zeros((16, LANES), jnp.bfloat16)
    one = jnp.ones((16, LANES), jnp.bfloat16)
    hit = [high == key for key in highs]
    values = [jnp.where(h, coarse, zero) for h in hit] + [jnp.where(h, fine, zero) for h in hit]
    one_hot = [jnp.where(low == key, one, zero) for key in lows]
    return jnp.concatenate(values, axis=0), jnp.concatenate(one_hot, axis=0)


def contract(slices):
    values = jnp.concatenate([s[0] for s in slices], axis=1)
    one_hot = jnp.concatenate([s[1] for s in slices], axis=1)
    return lax.dot_general(
        values, one_hot, (((1,), (1,)), ((), ())), preferred_element_type=jnp.float32
    )


def store_nodal(ref, lead, total, sign=1.0):
    high_total = total.shape[0] // 2
    both = (total[:high_total] + total[high_total:]) * sign
    half = high_total // 2
    ref[(*lead, slice(0, half), slice(0, LOW))] = both[:half]
    ref[(*lead, slice(0, half), slice(LOW, LANES))] = both[half:]


def packet_kernel(field, corners, motion, engaged, gaps, factor, out, corners_out):
    trace = []
    for body in range(2):
        picked = [
            lane_lookup(lambda r: wide(field, r, body), corners[body, c], 16) for c in range(3)
        ]
        trace.append((picked[0] + picked[1] + picked[2]) / 3.0)
    out[0, 0] = motion[...]
    out[0, 1] = trace[1]
    out[0, 2] = trace[0]
    out[0, 3] = engaged[...].astype(jnp.float32) * factor[...]
    out[0, 4] = gaps[2] + nitsche * (gaps[0] - gaps[1])
    corners_out[...] = corners[...]


def element_sum(field, vertices, entries, out, coarse_at, fine_at, body=0):
    highs = keys(32, True)
    lows = keys(LOW)
    total = jnp.zeros((64, LOW), jnp.float32)
    order = ((0, 4, 5, 6), (4, 1, 7, 8), (5, 7, 2, 9), (6, 8, 9, 3))
    for j in range(8):
        here = slice(ROWS * j, ROWS * (j + 1))
        corner = [vertices[body, pl.ds(32 * j + c, ROWS, stride=4), :] for c in range(4)]
        picked = [lane_lookup(lambda r: wide(field, r, body), i, 16) for i in corner]
        k = [entries[body, e, here, :] for e in range(10)]
        for c in range(4):
            o = order[c]
            row = (
                k[o[0]] * picked[0]
                + k[o[1]] * picked[1]
                + k[o[2]] * picked[2]
                + k[o[3]] * picked[3]
            )
            coarse, fine = split(row)
            coarse_at[body, c, here] = coarse
            fine_at[body, c, here] = fine
        slices = [
            scatter_operands(
                wide(vertices, 32 * j + 4 * s + c, body),
                wide(coarse_at, ROWS * j + s, body, c),
                wide(fine_at, ROWS * j + s, body, c),
                highs,
                lows,
            )
            for c in range(4)
            for s in range(ROWS)
        ]
        total = total + contract(slices)
    store_nodal(out, (), total, -1.0)


def disc_kernel(field, vertices, entries, partners, out, lookup, coarse_at, fine_at):
    for g in range(4):
        for s in range(ROWS):
            lookup[pl.ds(64 * g + s, ROWS, stride=ROWS), :] = partners[
                ROWS * g : ROWS * (g + 1), LANES * s : LANES * (s + 1)
            ]
    element_sum(field, vertices, entries, out, coarse_at, fine_at)


def rim_lookup(first_row, second_row, index):
    first = lane_lookup(first_row, index, 16)
    second = lane_lookup(second_row, index, 16)
    place = lax.broadcasted_iota(jnp.int32, (ROWS, LANES), 0)
    return jnp.where(place < 4, first, second)


def rim_slots(rims, slot_out):
    highs = keys(32, True)
    lows = keys(LOW)
    lane = lax.broadcasted_iota(jnp.int32, (ROWS, LANES), 1)
    for body in range(2):
        slices = []
        for s in range(4):
            coarse, fine = split((lane + (LANES * s + 1)).astype(jnp.float32))
            slices.append(scatter_operands(wide(rims, 4 * body + s), coarse, fine, highs, lows))
        store_nodal(slot_out, (body,), contract(slices))


def pad_kernel(
    field, vertices, entries, rims, whole, storage, disc,
    out, rim_out, rims_out, slot_out, field_out, storage_out, coarse_at, fine_at,
):
    rims_out[...] = rims[...]
    field_out[...] = whole[...]
    storage_out[...] = storage[...]
    rim_slots(rims, slot_out)
    element_sum(field, vertices, entries, out.at[1], coarse_at, fine_at)
    out[0] = disc[...]
    rim_out[...] = rim_lookup(lambda r: wide(out, r, 0), lambda r: wide(out, r, 1), rims[...])


def source_of(face, place):
    z = (face >> 2) + AHEAD[place % 8]
    near = (face & 3) ^ ((2 if place & 8 else 0) | (1 if place & 16 else 0))
    return ((z & 7) << 2) | near


def packet_work(face, packets, own, lookup, normal, trace, total, coarse_at, fine_at):
    highs = keys(16, True)
    lows = keys(LOW)
    mine = lookup[pl.ds(pl.multiple_of(face * ROWS, ROWS), ROWS), :]
    n = 0
    for ref, first in packets:
        for group in range(0, 8, 4):
            slices = []
            for at in range(group, group + 4):
                source = source_of(face, first + at)
                chosen = (mine >> 10) == source
                local = mine & 1023
                normal = jnp.where(chosen, lane_lookup(lambda r: wide(ref, r, at, 0), local, 8), normal)
                trace = jnp.where(chosen, lane_lookup(lambda r: wide(ref, r, at, 1), local, 8), trace)

                index = lookup[pl.ds(pl.multiple_of(source * ROWS, ROWS), ROWS), :]
                local = index & 1023
                pad_normal = lane_lookup(lambda r: wide(own, r, 0, 0), local, 8)
                pad_trace = lane_lookup(lambda r: wide(own, r, 0, 1), local, 8)
                rate = (
                    ref[at, 3]
                    * (film_floor + jnp.maximum(ref[at, 4] - nitsche * pad_normal, 0.0))
                    * (pad_trace - ref[at, 2])
                )
                coarse, fine = split(jnp.where((index >> 10) == face, rate, 0.0))
                coarse_at[n] = coarse
                fine_at[n] = fine
                slices += [
                    scatter_operands(
                        wide(lookup, source * ROWS + s) & 1023,
                        wide(coarse_at, s, n),
                        wide(fine_at, s, n),
                        highs,
                        lows,
                    )
                    for s in range(ROWS)
                ]
                n += 1
            total = total + contract(slices)
    return normal, trace, total


def first_kernel(eight, twin, lookup, own, normal_out, trace_out, total_out, coarse_at, fine_at):
    zero = jnp.zeros((ROWS, LANES), jnp.float32)
    normal_out[...], trace_out[...], total_out[...] = packet_work(
        lax.axis_index("face"), ((eight, 0), (twin, 16)), own, lookup,
        zero, zero, jnp.zeros((32, LOW), jnp.float32), coarse_at, fine_at,
    )


def second_kernel(
    other, lookup, own, normal, trace, total, normal_out, trace_out, total_out, coarse_at, fine_at
):
    normal_out[...], trace_out[...], total_out[...] = packet_work(
        lax.axis_index("face"), ((other, 8),), own, lookup,
        normal[...], trace[...], total[...], coarse_at, fine_at,
    )


def contact_kernel(
    last, lookup, own, normal, trace, total, corners, rims, element,
    pressure_out, nodal, rim_out, pads, coarse_at, fine_at,
):
    pad_normal, pad_trace, total = packet_work(
        lax.axis_index("face"), ((last, 24),), own, lookup,
        normal[...], trace[...], total[...], coarse_at, fine_at,
    )
    weight = own[0, 3]
    pressure = jnp.where(
        weight != 0.0, jnp.maximum(own[0, 4] - nitsche * pad_normal, 0.0), 0.0
    )
    pressure_out[...] = pressure
    disc_rate = weight * (film_floor + pressure) * (pad_trace - own[0, 2])
    store_nodal(pads, (), total, -1.0)

    highs = keys(32, True)
    lows = keys(LOW)
    for body in range(2):
        rate = disc_rate if body == 0 else pads[...]
        coarse, fine = split(rate / 3.0)
        at = 8 + body
        coarse_at[at] = coarse
        fine_at[at] = fine
        slices = [
            scatter_operands(
                wide(corners, s, body, c), wide(coarse_at, s, at), wide(fine_at, s, at), highs, lows
            )
            for c in range(3)
            for s in range(ROWS)
        ]
        store_nodal(nodal, (body,), contract(slices))
        nodal[body] = nodal[body] + element[body]
    rim_out[...] = rim_lookup(lambda r: wide(nodal, r, 0), lambda r: wide(nodal, r, 1), rims[...])


def inner_kernel(
    field, vertices, entries, rims, storage, partners, engaged, gaps, motion,
    out, rim_out, slot_out, field_out, storage_out, mine, active, gaps_out, normals, coarse_at, fine_at,
):
    field_out[...] = field[...]
    storage_out[...] = storage[...]
    active[...] = engaged[...].astype(jnp.float32)
    gaps_out[...] = gaps[...]
    for patch in range(32):
        normals[patch] = motion[...]
    face = lax.axis_index("face")
    place = lax.broadcasted_iota(jnp.int32, (ROWS, LANES), 0)
    faces = jnp.zeros((ROWS, LANES), jnp.int32)
    for s in range(ROWS):
        block = partners[
            pl.ds(pl.multiple_of(face & -ROWS, ROWS), ROWS), LANES * s : LANES * (s + 1)
        ]
        row = jnp.sum(jnp.where(place == (face & (ROWS - 1)), block, 0), axis=0, keepdims=True)
        faces = jnp.where(place == s, row, faces)
    mine[...] = faces
    rim_slots(rims, slot_out)
    for body in range(2):
        element_sum(field, vertices, entries, out.at[body], coarse_at, fine_at, body)
    rim_out[...] = rim_lookup(lambda r: wide(out, r, 0), lambda r: wide(out, r, 1), rims[...])


def pressure_kernel(normals, mine, active, gaps, out):
    patch = mine[...] >> 10
    local = mine[...] & 1023
    normal = jnp.zeros((ROWS, LANES), jnp.float32)
    for source in range(32):
        found = lane_lookup(lambda r: wide(normals, r, source), local, 8)
        normal = jnp.where(patch == source, found, normal)
    out[...] = active[...] * jnp.maximum(gaps[2] + nitsche * (gaps[0] - normal - gaps[1]), 0.0)


def advance_kernel(field, storage, nodal, slots, early, late, out, gained):
    place = lax.broadcasted_iota(jnp.int32, (ROWS, LANES), 0)
    depth = lax.axis_index("depth")
    even = (depth & 1) == 0
    other = jnp.where((depth > 0) & (depth < 7), early[...], 0.0)
    above = jnp.where(even, late[...], other)
    below = jnp.where(even, other, late[...])
    gained[...] = jnp.where((place & 1) == 0, pltpu.roll(below, 7, 0), pltpu.roll(above, 1, 0))
    for body in range(2):
        for half in range(2):
            here = slice(ROWS * half, ROWS * (half + 1))
            slot = slots[body, here].astype(jnp.int32)
            found = lane_lookup(
                lambda r: wide(gained, 4 * body + r), jnp.maximum(slot - 1, 0), 4
            )
            total = nodal[body, here] + jnp.where(slot > 0, found, 0.0)
            out[body, here] = field[body, here] + increment_factor * total / storage[body, here]


def here(*shape, dtype=jnp.float32):
    return pltpu.VMEM(shape, dtype)


class Placed:
    def __init__(self, array, near):
        self.array, self.near = array, near

    @staticmethod
    def of(argument):
        return argument if isinstance(argument, Placed) else Placed(argument, False)


def near(array):
    return Placed(array, True)


def one_body(array, body):
    block = (1,) + array.shape[1:]
    return pl.BlockSpec(block, lambda i: (body,) + (0,) * (len(block) - 1), memory_space=pltpu.VMEM)


def call(body, out, arguments, scratch=(), specs=None, name=None, time=1.0):
    whole = pl.BlockSpec(memory_space=pltpu.VMEM)
    specs = specs or {}
    arguments = tuple(
        pltpu.with_memory_space_constraint(a.array, pltpu.VMEM if a.near else pltpu.HBM)
        for a in map(Placed.of, arguments)
    )
    return pl.pallas_call(
        body,
        out_shape=out,
        in_specs=[specs.get(i, whole) for i in range(len(arguments))],
        out_specs=jax.tree.map(lambda _: whole, out),
        scratch_shapes=[pltpu.VMEM(s, jnp.float32) for s in scratch],
        grid=(1,) if specs else (),
        name=name,
        cost_estimate=pl.CostEstimate(
            flops=0, transcendentals=0, bytes_accessed=int(time * 3.6e6)
        ),
    )(*arguments)


def local(
    thermal_field,
    lumped_storage,
    simplex_vertices,
    stiffness_entries,
    interface_vertices,
    touching_triangle_vertices,
    partner_lookup,
    engaged_flags,
    rotor_gap_quantities,
    lining_orthogonal_motion,
    touching_transfer_factor,
):
    field = thermal_field.reshape(2, 16, LANES)
    storage = lumped_storage.reshape(2, 16, LANES)
    vertices = simplex_vertices.reshape(2, 4, 64, LANES).transpose(0, 2, 1, 3).reshape(2, 256, LANES)
    entries = stiffness_entries.reshape(2, 10, 64, LANES)
    rims = interface_vertices.reshape(2, 2, 2, LANES).transpose(0, 2, 1, 3).reshape(8, LANES)
    corners = touching_triangle_vertices.reshape(2, 3, ROWS, LANES)
    engaged = engaged_flags.reshape(ROWS, LANES)
    gaps = rotor_gap_quantities.reshape(3, ROWS, LANES)
    motion = lining_orthogonal_motion.reshape(ROWS, LANES)
    factor = touching_transfer_factor.reshape(ROWS, LANES)
    tile = here(ROWS, LANES)
    nodes = here(16, LANES)
    sums = (tile, tile, here(32, LOW))

    def along(cells, step):
        return lax.ppermute(cells, "face", [(i, (i + 4 * step) % 32) for i in range(32)])

    def across(cells, bit):
        return lax.ppermute(cells, "face", [(i, i ^ bit) for i in range(32)])

    def of_body(body):
        return {k: one_body(a, body) for k, a in enumerate((field, vertices, entries))}

    parts = ((1, 4, 64, LANES),) * 2

    def elements_and_eight(own):
        behind = along(own, 1)
        ahead = along(own, -1)
        disc, lookup = call(
            disc_kernel,
            (nodes, here(256, LANES, dtype=jnp.int32)),
            (field, vertices, entries, partner_lookup),
            scratch=parts,
            specs=of_body(0),
            name="disc_element",
            time=2.2,
        )
        behind, ahead, disc, lookup = lax.optimization_barrier((behind, ahead, disc, lookup))
        three = jnp.concatenate([behind, own, ahead], axis=0)
        three, again = lax.optimization_barrier((three, field))
        far_behind = along(three, 3)
        far_ahead = along(three[:2], -3)
        element, rim_element, rims_near, *kept = call(
            pad_kernel,
            (here(2, 16, LANES), tile, here(ROWS, LANES, dtype=jnp.int32))
            + (here(2, 16, LANES),) * 3,
            (again, vertices, entries, rims, field, storage, near(disc)),
            scratch=parts,
            specs=of_body(1),
            name="pad_element",
            time=2.5,
        )
        far_behind, far_ahead, element, rim_element = lax.optimization_barrier(
            (far_behind, far_ahead, element, rim_element)
        )
        eight = jnp.concatenate([three, far_behind, far_ahead], axis=0)
        return eight, lookup, element, rim_element, rims_near, kept

    def surface_block():
        own, own_corners = call(
            packet_kernel,
            (here(1, 5, ROWS, LANES), here(2, 3, ROWS, LANES, dtype=jnp.int32)),
            (field, corners, motion, engaged, gaps, factor),
            name="packet",
        )
        eight, lookup, element, rim_element, rims_near, kept = elements_and_eight(own)
        other = across(eight, 2)
        twin = across(eight, 1)
        done = call(
            first_kernel,
            sums,
            (near(eight), near(twin), near(lookup), near(own)),
            scratch=((16, ROWS, LANES), (16, ROWS, LANES)),
            name="first_packets",
            time=1.5,
        )
        other, done = lax.optimization_barrier((other, done))
        last = across(other, 1)
        done = call(
            second_kernel,
            sums,
            (near(other), near(lookup), near(own), *map(near, done)),
            scratch=((8, ROWS, LANES), (8, ROWS, LANES)),
            name="second_packets",
        )
        last, done = lax.optimization_barrier((last, done))
        pressure, nodal, rim_total = call(
            contact_kernel,
            (tile, here(2, 16, LANES), tile),
            tuple(map(near, (last, lookup, own, *done, own_corners, rims_near, element))),
            scratch=((ROWS, LANES), (10, ROWS, LANES), (10, ROWS, LANES)),
            name="contact",
            time=1.5,
        )
        return pressure, nodal, rim_total, rim_element, *kept

    def inner_block():
        element, rim_element, *kept, mine, active, gaps_near, normals = call(
            inner_kernel,
            (here(2, 16, LANES), tile)
            + (here(2, 16, LANES),) * 3
            + (here(ROWS, LANES, dtype=jnp.int32), tile, here(3, ROWS, LANES), here(32, ROWS, LANES)),
            (field, vertices, entries, rims, storage, partner_lookup, engaged, gaps, motion),
            scratch=((2, 4, 64, LANES),) * 2,
            name="inner_elements",
            time=4.5,
        )
        early = lax.ppermute(rim_element, "depth", [(1, 2), (2, 1), (3, 4), (4, 3), (5, 6), (6, 5)])
        normals = lax.all_to_all(normals, "face", 0, 0, tiled=True)
        pressure = call(
            pressure_kernel,
            tile,
            tuple(map(near, (normals, mine, active, gaps_near))),
            name="pressure",
        )
        return pressure, element, rim_element, early, *kept

    pressure, nodal, rim_total, early, slots, field_near, storage_near = lax.cond(
        lax.axis_index("depth") == 0, surface_block, inner_block
    )
    late = lax.ppermute(rim_total, "depth", [(i, i ^ 1) for i in range(8)])
    advanced = call(
        advance_kernel,
        jax.ShapeDtypeStruct((2, 16, LANES), jnp.float32),
        tuple(map(near, (field_near, storage_near, nodal, slots, early, late))),
        scratch=((ROWS, LANES),),
        name="advance",
    )
    return advanced.reshape(thermal_field.shape), pressure.reshape(1, 1024)


def solution(mesh):
    placed = (
        P(None, "face", "depth", None),
        P(None, "face", "depth", None),
        P(None, "face", "depth", None, None),
        P(None, "face", "depth", None, None),
        P(None, "face", "depth", None, None),
        P(None, "face", None, None),
        P(),
        P("face", None),
        P(None, "face", None),
        P("face", None),
        P("face", None),
    )
    return jax.shard_map(
        local,
        mesh=mesh,
        in_specs=placed,
        out_specs=(P(None, "face", "depth", None), P("face", None)),
        check_vma=False,
    )
```

```python
import functools

import jax
import jax.numpy as jnp
from jax import lax
from jax.experimental import pallas as pl
from jax.experimental.pallas import tpu as pltpu
from jax.sharding import PartitionSpec as P

increment_factor = 0.05
nitsche = 1.0
film_floor = 0.25

LANES = 128
ROWS = 8
LOW = 64
AHEAD = (-1, 0, 1, 2, 3, 4, -3, -2)


def lane_lookup(row_of, indices, row_total):
    lane = indices & (LANES - 1)
    row = indices >> 7
    level = [
        jnp.take_along_axis(row_of(r), lane, axis=1, mode="promise_in_bounds")
        for r in range(row_total)
    ]
    bit = 0
    while len(level) > 1:
        odd = ((row >> bit) & 1) == 1
        level = [jnp.where(odd, level[k + 1], level[k]) for k in range(0, len(level), 2)]
        bit += 1
    return level[0]


def wide(ref, row, *lead):
    return ref[(*lead, pl.ds(row, ROWS, stride=0), slice(None))]


def split(values):
    coarse = values.astype(jnp.bfloat16).astype(jnp.float32)
    fine = (values - coarse).astype(jnp.bfloat16).astype(jnp.float32)
    return coarse, fine


def double(tile):
    return jnp.concatenate([tile, tile], axis=0).astype(jnp.bfloat16)


def keys(total, interleaved=False):
    out = []
    for k in range(total // 16):
        halves = []
        for h in range(2):
            place = lax.broadcasted_iota(jnp.int32, (ROWS, LANES), 0) + (16 * k + ROWS * h)
            if interleaved:
                place = (place % (total // 2)) * 2 + place // (total // 2)
            halves.append(place.astype(jnp.float32))
        out.append(jnp.concatenate(halves, axis=0).astype(jnp.bfloat16))
    return out


def scatter_operands(index, coarse, fine, highs, lows):
    high = double((index >> 6).astype(jnp.float32))
    low = double((index & (LOW - 1)).astype(jnp.float32))
    coarse = double(coarse)
    fine = double(fine)
    zero = jnp.zeros((16, LANES), jnp.bfloat16)
    one = jnp.ones((16, LANES), jnp.bfloat16)
    hit = [high == key for key in highs]
    values = [jnp.where(h, coarse, zero) for h in hit] + [jnp.where(h, fine, zero) for h in hit]
    one_hot = [jnp.where(low == key, one, zero) for key in lows]
    return jnp.concatenate(values, axis=0), jnp.concatenate(one_hot, axis=0)


def contract(slices):
    values = jnp.concatenate([s[0] for s in slices], axis=1)
    one_hot = jnp.concatenate([s[1] for s in slices], axis=1)
    return lax.dot_general(
        values, one_hot, (((1,), (1,)), ((), ())), preferred_element_type=jnp.float32
    )


def store_nodal(ref, lead, total, sign=1.0):
    high_total = total.shape[0] // 2
    both = (total[:high_total] + total[high_total:]) * sign
    half = high_total // 2
    ref[(*lead, slice(0, half), slice(0, LOW))] = both[:half]
    ref[(*lead, slice(0, half), slice(LOW, LANES))] = both[half:]


def packet_kernel(field, corners, motion, engaged, gaps, factor, out, corners_out):
    trace = []
    for body in range(2):
        picked = [
            lane_lookup(lambda r: wide(field, r, body), corners[body, c], 16) for c in range(3)
        ]
        trace.append((picked[0] + picked[1] + picked[2]) / 3.0)
    out[0, 0] = motion[...]
    out[0, 1] = trace[1]
    out[0, 2] = trace[0]
    out[0, 3] = engaged[...].astype(jnp.float32) * factor[...]
    out[0, 4] = gaps[2] + nitsche * (gaps[0] - gaps[1])
    corners_out[...] = corners[...]


def element_sum(field, vertices, entries, out, coarse_at, fine_at, body=0):
    highs = keys(32, True)
    lows = keys(LOW)
    total = jnp.zeros((64, LOW), jnp.float32)
    order = ((0, 4, 5, 6), (4, 1, 7, 8), (5, 7, 2, 9), (6, 8, 9, 3))
    for j in range(8):
        here = slice(ROWS * j, ROWS * (j + 1))
        corner = [vertices[body, pl.ds(32 * j + c, ROWS, stride=4), :] for c in range(4)]
        picked = [lane_lookup(lambda r: wide(field, r, body), i, 16) for i in corner]
        k = [entries[body, e, here, :] for e in range(10)]
        for c in range(4):
            o = order[c]
            row = (
                k[o[0]] * picked[0]
                + k[o[1]] * picked[1]
                + k[o[2]] * picked[2]
                + k[o[3]] * picked[3]
            )
            coarse, fine = split(row)
            coarse_at[body, c, here] = coarse
            fine_at[body, c, here] = fine
        slices = [
            scatter_operands(
                wide(vertices, 32 * j + 4 * s + c, body),
                wide(coarse_at, ROWS * j + s, body, c),
                wide(fine_at, ROWS * j + s, body, c),
                highs,
                lows,
            )
            for c in range(4)
            for s in range(ROWS)
        ]
        total = total + contract(slices)
    store_nodal(out, (), total, -1.0)


def disc_kernel(field, vertices, entries, partners, out, lookup, coarse_at, fine_at):
    for g in range(4):
        for s in range(ROWS):
            lookup[pl.ds(64 * g + s, ROWS, stride=ROWS), :] = partners[
                ROWS * g : ROWS * (g + 1), LANES * s : LANES * (s + 1)
            ]
    element_sum(field, vertices, entries, out, coarse_at, fine_at)


def rim_lookup(first_row, second_row, index):
    first = lane_lookup(first_row, index, 16)
    second = lane_lookup(second_row, index, 16)
    place = lax.broadcasted_iota(jnp.int32, (ROWS, LANES), 0)
    return jnp.where(place < 4, first, second)


def rim_slots(rims, slot_out):
    highs = keys(32, True)
    lows = keys(LOW)
    lane = lax.broadcasted_iota(jnp.int32, (ROWS, LANES), 1)
    for body in range(2):
        slices = []
        for s in range(4):
            coarse, fine = split((lane + (LANES * s + 1)).astype(jnp.float32))
            slices.append(scatter_operands(wide(rims, 4 * body + s), coarse, fine, highs, lows))
        store_nodal(slot_out, (body,), contract(slices))


def pad_kernel(
    field, vertices, entries, rims, whole, storage, disc,
    out, rim_out, rims_out, slot_out, field_out, storage_out, coarse_at, fine_at,
):
    rims_out[...] = rims[...]
    field_out[...] = whole[...]
    storage_out[...] = storage[...]
    rim_slots(rims, slot_out)
    element_sum(field, vertices, entries, out.at[1], coarse_at, fine_at)
    out[0] = disc[...]
    rim_out[...] = rim_lookup(lambda r: wide(out, r, 0), lambda r: wide(out, r, 1), rims[...])


def source_of(face, place):
    z = (face >> 2) + AHEAD[place % 8]
    near = (face & 3) ^ ((2 if place & 8 else 0) | (1 if place & 16 else 0))
    return ((z & 7) << 2) | near


def packet_work(face, packets, own, lookup, normal, trace, total, coarse_at, fine_at):
    highs = keys(16, True)
    lows = keys(LOW)
    mine = lookup[pl.ds(pl.multiple_of(face * ROWS, ROWS), ROWS), :]
    n = 0
    for ref, first, count in packets:
        for group in range(0, count, 4):
            slices = []
            for at in range(group, min(group + 4, count)):
                source = source_of(face, first + at)
                chosen = (mine >> 10) == source
                local = mine & 1023
                normal = jnp.where(chosen, lane_lookup(lambda r: wide(ref, r, at, 0), local, 8), normal)
                trace = jnp.where(chosen, lane_lookup(lambda r: wide(ref, r, at, 1), local, 8), trace)

                index = lookup[pl.ds(pl.multiple_of(source * ROWS, ROWS), ROWS), :]
                local = index & 1023
                pad_normal = lane_lookup(lambda r: wide(own, r, 0, 0), local, 8)
                pad_trace = lane_lookup(lambda r: wide(own, r, 0, 1), local, 8)
                rate = (
                    ref[at, 3]
                    * (film_floor + jnp.maximum(ref[at, 4] - nitsche * pad_normal, 0.0))
                    * (pad_trace - ref[at, 2])
                )
                coarse, fine = split(jnp.where((index >> 10) == face, rate, 0.0))
                coarse_at[n] = coarse
                fine_at[n] = fine
                slices += [
                    scatter_operands(
                        wide(lookup, source * ROWS + s) & 1023,
                        wide(coarse_at, s, n),
                        wide(fine_at, s, n),
                        highs,
                        lows,
                    )
                    for s in range(ROWS)
                ]
                n += 1
            total = total + contract(slices)
    return normal, trace, total


def first_kernel(eight, twin, three, lookup, own, normal_out, trace_out, total_out, coarse_at, fine_at):
    zero = jnp.zeros((ROWS, LANES), jnp.float32)
    normal_out[...], trace_out[...], total_out[...] = packet_work(
        lax.axis_index("face"), ((eight, 0, 8), (twin, 16, 8), (three, 8, 3)), own, lookup,
        zero, zero, jnp.zeros((32, LOW), jnp.float32), coarse_at, fine_at,
    )


def second_kernel(
    three, five, lookup, own, normal, trace, total, normal_out, trace_out, total_out, coarse_at, fine_at
):
    normal_out[...], trace_out[...], total_out[...] = packet_work(
        lax.axis_index("face"), ((three, 24, 3), (five, 11, 5)), own, lookup,
        normal[...], trace[...], total[...], coarse_at, fine_at,
    )


def contact_kernel(
    last, lookup, own, normal, trace, total, corners, rims, element,
    pressure_out, nodal, rim_out, pads, coarse_at, fine_at,
):
    pad_normal, pad_trace, total = packet_work(
        lax.axis_index("face"), ((last, 27, 5),), own, lookup,
        normal[...], trace[...], total[...], coarse_at, fine_at,
    )
    weight = own[0, 3]
    pressure = jnp.where(
        weight != 0.0, jnp.maximum(own[0, 4] - nitsche * pad_normal, 0.0), 0.0
    )
    pressure_out[...] = pressure
    disc_rate = weight * (film_floor + pressure) * (pad_trace - own[0, 2])
    store_nodal(pads, (), total, -1.0)

    highs = keys(32, True)
    lows = keys(LOW)
    for body in range(2):
        rate = disc_rate if body == 0 else pads[...]
        coarse, fine = split(rate / 3.0)
        at = 8 + body
        coarse_at[at] = coarse
        fine_at[at] = fine
        slices = [
            scatter_operands(
                wide(corners, s, body, c), wide(coarse_at, s, at), wide(fine_at, s, at), highs, lows
            )
            for c in range(3)
            for s in range(ROWS)
        ]
        store_nodal(nodal, (body,), contract(slices))
        nodal[body] = nodal[body] + element[body]
    rim_out[...] = rim_lookup(lambda r: wide(nodal, r, 0), lambda r: wide(nodal, r, 1), rims[...])


def inner_kernel(
    field, vertices, entries, rims, storage, partners, engaged, gaps, motion,
    out, rim_out, slot_out, field_out, storage_out, mine, active, gaps_out, normals, coarse_at, fine_at,
):
    field_out[...] = field[...]
    storage_out[...] = storage[...]
    active[...] = engaged[...].astype(jnp.float32)
    gaps_out[...] = gaps[...]
    for patch in range(32):
        normals[patch] = motion[...]
    face = lax.axis_index("face")
    place = lax.broadcasted_iota(jnp.int32, (ROWS, LANES), 0)
    faces = jnp.zeros((ROWS, LANES), jnp.int32)
    for s in range(ROWS):
        block = partners[
            pl.ds(pl.multiple_of(face & -ROWS, ROWS), ROWS), LANES * s : LANES * (s + 1)
        ]
        row = jnp.sum(jnp.where(place == (face & (ROWS - 1)), block, 0), axis=0, keepdims=True)
        faces = jnp.where(place == s, row, faces)
    mine[...] = faces
    rim_slots(rims, slot_out)
    for body in range(2):
        element_sum(field, vertices, entries, out.at[body], coarse_at, fine_at, body)
    rim_out[...] = rim_lookup(lambda r: wide(out, r, 0), lambda r: wide(out, r, 1), rims[...])


def pressure_kernel(normals, mine, active, gaps, out):
    patch = mine[...] >> 10
    local = mine[...] & 1023
    normal = jnp.zeros((ROWS, LANES), jnp.float32)
    for source in range(32):
        found = lane_lookup(lambda r: wide(normals, r, source), local, 8)
        normal = jnp.where(patch == source, found, normal)
    out[...] = active[...] * jnp.maximum(gaps[2] + nitsche * (gaps[0] - normal - gaps[1]), 0.0)


def advance_kernel(field, storage, nodal, slots, early, late, out, gained):
    place = lax.broadcasted_iota(jnp.int32, (ROWS, LANES), 0)
    depth = lax.axis_index("depth")
    even = (depth & 1) == 0
    other = jnp.where((depth > 0) & (depth < 7), early[...], 0.0)
    above = jnp.where(even, late[...], other)
    below = jnp.where(even, other, late[...])
    gained[...] = jnp.where((place & 1) == 0, pltpu.roll(below, 7, 0), pltpu.roll(above, 1, 0))
    for body in range(2):
        for half in range(2):
            here = slice(ROWS * half, ROWS * (half + 1))
            slot = slots[body, here].astype(jnp.int32)
            found = lane_lookup(
                lambda r: wide(gained, 4 * body + r), jnp.maximum(slot - 1, 0), 4
            )
            total = nodal[body, here] + jnp.where(slot > 0, found, 0.0)
            out[body, here] = field[body, here] + increment_factor * total / storage[body, here]


def here(*shape, dtype=jnp.float32):
    return pltpu.VMEM(shape, dtype)


class Placed:
    def __init__(self, array, near):
        self.array, self.near = array, near

    @staticmethod
    def of(argument):
        return argument if isinstance(argument, Placed) else Placed(argument, False)


def near(array):
    return Placed(array, True)


def one_body(array, body):
    block = (1,) + array.shape[1:]
    return pl.BlockSpec(block, lambda i: (body,) + (0,) * (len(block) - 1), memory_space=pltpu.VMEM)


def call(body, out, arguments, scratch=(), specs=None, name=None, time=1.0):
    whole = pl.BlockSpec(memory_space=pltpu.VMEM)
    specs = specs or {}
    arguments = tuple(
        pltpu.with_memory_space_constraint(a.array, pltpu.VMEM if a.near else pltpu.HBM)
        for a in map(Placed.of, arguments)
    )
    return pl.pallas_call(
        body,
        out_shape=out,
        in_specs=[specs.get(i, whole) for i in range(len(arguments))],
        out_specs=jax.tree.map(lambda _: whole, out),
        scratch_shapes=[pltpu.VMEM(s, jnp.float32) for s in scratch],
        grid=(1,) if specs else (),
        name=name,
        cost_estimate=pl.CostEstimate(
            flops=0, transcendentals=0, bytes_accessed=int(time * 3.6e6)
        ),
    )(*arguments)


def local(
    thermal_field,
    lumped_storage,
    simplex_vertices,
    stiffness_entries,
    interface_vertices,
    touching_triangle_vertices,
    partner_lookup,
    engaged_flags,
    rotor_gap_quantities,
    lining_orthogonal_motion,
    touching_transfer_factor,
):
    field = thermal_field.reshape(2, 16, LANES)
    storage = lumped_storage.reshape(2, 16, LANES)
    vertices = simplex_vertices.reshape(2, 4, 64, LANES).transpose(0, 2, 1, 3).reshape(2, 256, LANES)
    entries = stiffness_entries.reshape(2, 10, 64, LANES)
    rims = interface_vertices.reshape(2, 2, 2, LANES).transpose(0, 2, 1, 3).reshape(8, LANES)
    corners = touching_triangle_vertices.reshape(2, 3, ROWS, LANES)
    engaged = engaged_flags.reshape(ROWS, LANES)
    gaps = rotor_gap_quantities.reshape(3, ROWS, LANES)
    motion = lining_orthogonal_motion.reshape(ROWS, LANES)
    factor = touching_transfer_factor.reshape(ROWS, LANES)
    tile = here(ROWS, LANES)
    nodes = here(16, LANES)
    sums = (tile, tile, here(32, LOW))

    def along(cells, step):
        return lax.ppermute(cells, "face", [(i, (i + 4 * step) % 32) for i in range(32)])

    def across(cells, bit):
        return lax.ppermute(cells, "face", [(i, i ^ bit) for i in range(32)])

    def of_body(body):
        return {k: one_body(a, body) for k, a in enumerate((field, vertices, entries))}

    parts = ((1, 4, 64, LANES),) * 2

    def elements_and_eight(own):
        behind = along(own, 1)
        ahead = along(own, -1)
        disc, lookup = call(
            disc_kernel,
            (nodes, here(256, LANES, dtype=jnp.int32)),
            (field, vertices, entries, partner_lookup),
            scratch=parts,
            specs=of_body(0),
            name="disc_element",
            time=2.2,
        )
        behind, ahead, disc, lookup = lax.optimization_barrier((behind, ahead, disc, lookup))
        three = jnp.concatenate([behind, own, ahead], axis=0)
        three, again = lax.optimization_barrier((three, field))
        far_ahead = along(three, -3)
        far_behind = along(three[:2], 2)
        other_three = across(three, 2)
        element, rim_element, rims_near, *kept = call(
            pad_kernel,
            (here(2, 16, LANES), tile, here(ROWS, LANES, dtype=jnp.int32))
            + (here(2, 16, LANES),) * 3,
            (again, vertices, entries, rims, field, storage, near(disc)),
            scratch=parts,
            specs=of_body(1),
            name="pad_element",
            time=2.5,
        )
        far_behind, far_ahead, element, rim_element = lax.optimization_barrier(
            (far_behind, far_ahead, element, rim_element)
        )
        five = jnp.concatenate([far_ahead, far_behind], axis=0)
        eight = jnp.concatenate([three, five], axis=0)
        return eight, five, other_three, lookup, element, rim_element, rims_near, kept

    def surface_block():
        own, own_corners = call(
            packet_kernel,
            (here(1, 5, ROWS, LANES), here(2, 3, ROWS, LANES, dtype=jnp.int32)),
            (field, corners, motion, engaged, gaps, factor),
            name="packet",
        )
        eight, five, other_three, lookup, element, rim_element, rims_near, kept = (
            elements_and_eight(own)
        )
        other_five = across(five, 2)
        twin = across(eight, 1)
        last_three = across(other_three, 1)
        done = call(
            first_kernel,
            sums,
            (near(eight), near(twin), near(other_three), near(lookup), near(own)),
            scratch=((19, ROWS, LANES),) * 2,
            name="first_packets",
            time=1.5,
        )
        other_five, last_three, done = lax.optimization_barrier((other_five, last_three, done))
        last = across(other_five, 1)
        done = call(
            second_kernel,
            sums,
            (near(last_three), near(other_five), near(lookup), near(own), *map(near, done)),
            scratch=((8, ROWS, LANES),) * 2,
            name="second_packets",
        )
        last, done = lax.optimization_barrier((last, done))
        pressure, nodal, rim_total = call(
            contact_kernel,
            (tile, here(2, 16, LANES), tile),
            tuple(map(near, (last, lookup, own, *done, own_corners, rims_near, element))),
            scratch=((ROWS, LANES), (10, ROWS, LANES), (10, ROWS, LANES)),
            name="contact",
            time=1.5,
        )
        return pressure, nodal, rim_total, rim_element, *kept

    def inner_block():
        element, rim_element, *kept, mine, active, gaps_near, normals = call(
            inner_kernel,
            (here(2, 16, LANES), tile)
            + (here(2, 16, LANES),) * 3
            + (here(ROWS, LANES, dtype=jnp.int32), tile, here(3, ROWS, LANES), here(32, ROWS, LANES)),
            (field, vertices, entries, rims, storage, partner_lookup, engaged, gaps, motion),
            scratch=((2, 4, 64, LANES),) * 2,
            name="inner_elements",
            time=4.5,
        )
        early = lax.ppermute(rim_element, "depth", [(1, 2), (2, 1), (3, 4), (4, 3), (5, 6), (6, 5)])
        normals = lax.all_to_all(normals, "face", 0, 0, tiled=True)
        pressure = call(
            pressure_kernel,
            tile,
            tuple(map(near, (normals, mine, active, gaps_near))),
            name="pressure",
        )
        return pressure, element, rim_element, early, *kept

    pressure, nodal, rim_total, early, slots, field_near, storage_near = lax.cond(
        lax.axis_index("depth") == 0, surface_block, inner_block
    )
    late = lax.ppermute(rim_total, "depth", [(i, i ^ 1) for i in range(8)])
    advanced = call(
        advance_kernel,
        jax.ShapeDtypeStruct((2, 16, LANES), jnp.float32),
        tuple(map(near, (field_near, storage_near, nodal, slots, early, late))),
        scratch=((ROWS, LANES),),
        name="advance",
    )
    return advanced.reshape(thermal_field.shape), pressure.reshape(1, 1024)


def solution(mesh):
    placed = (
        P(None, "face", "depth", None),
        P(None, "face", "depth", None),
        P(None, "face", "depth", None, None),
        P(None, "face", "depth", None, None),
        P(None, "face", "depth", None, None),
        P(None, "face", None, None),
        P(),
        P("face", None),
        P(None, "face", None),
        P("face", None),
        P("face", None),
    )
    return jax.shard_map(
        local,
        mesh=mesh,
        in_specs=placed,
        out_specs=(P(None, "face", "depth", None), P("face", None)),
        check_vma=False,
    )
```

```python
import functools

import jax
import jax.numpy as jnp
from jax import lax
from jax.experimental import pallas as pl
from jax.experimental.pallas import tpu as pltpu
from jax.sharding import PartitionSpec as P

increment_factor = 0.05
nitsche = 1.0
film_floor = 0.25

LANES = 128
ROWS = 8
DISC_FIRST = 6
LOW = 64
AHEAD = (-1, 0, 1, 2, 3, 4, -3, -2)


def lane_lookup(row_of, indices, row_total):
    lane = indices & (LANES - 1)
    row = indices >> 7
    level = [
        jnp.take_along_axis(row_of(r), lane, axis=1, mode="promise_in_bounds")
        for r in range(row_total)
    ]
    bit = 0
    while len(level) > 1:
        odd = ((row >> bit) & 1) == 1
        level = [jnp.where(odd, level[k + 1], level[k]) for k in range(0, len(level), 2)]
        bit += 1
    return level[0]


def wide(ref, row, *lead):
    return ref[(*lead, pl.ds(row, ROWS, stride=0), slice(None))]


def split(values):
    coarse = values.astype(jnp.bfloat16).astype(jnp.float32)
    fine = (values - coarse).astype(jnp.bfloat16).astype(jnp.float32)
    return coarse, fine


def double(tile):
    return jnp.concatenate([tile, tile], axis=0).astype(jnp.bfloat16)


def keys(total, interleaved=False):
    out = []
    for k in range(total // 16):
        halves = []
        for h in range(2):
            place = lax.broadcasted_iota(jnp.int32, (ROWS, LANES), 0) + (16 * k + ROWS * h)
            if interleaved:
                place = (place % (total // 2)) * 2 + place // (total // 2)
            halves.append(place.astype(jnp.float32))
        out.append(jnp.concatenate(halves, axis=0).astype(jnp.bfloat16))
    return out


def scatter_operands(index, coarse, fine, highs, lows):
    high = double((index >> 6).astype(jnp.float32))
    low = double((index & (LOW - 1)).astype(jnp.float32))
    coarse = double(coarse)
    fine = double(fine)
    zero = jnp.zeros((16, LANES), jnp.bfloat16)
    one = jnp.ones((16, LANES), jnp.bfloat16)
    hit = [high == key for key in highs]
    values = [jnp.where(h, coarse, zero) for h in hit] + [jnp.where(h, fine, zero) for h in hit]
    one_hot = [jnp.where(low == key, one, zero) for key in lows]
    return jnp.concatenate(values, axis=0), jnp.concatenate(one_hot, axis=0)


def contract(slices):
    values = jnp.concatenate([s[0] for s in slices], axis=1)
    one_hot = jnp.concatenate([s[1] for s in slices], axis=1)
    return lax.dot_general(
        values, one_hot, (((1,), (1,)), ((), ())), preferred_element_type=jnp.float32
    )


def store_nodal(ref, lead, total, sign=1.0):
    high_total = total.shape[0] // 2
    both = (total[:high_total] + total[high_total:]) * sign
    half = high_total // 2
    ref[(*lead, slice(0, half), slice(0, LOW))] = both[:half]
    ref[(*lead, slice(0, half), slice(LOW, LANES))] = both[half:]


def packet_kernel(field, corners, motion, engaged, gaps, factor, out, corners_out):
    trace = []
    for body in range(2):
        picked = [
            lane_lookup(lambda r: wide(field, r, body), corners[body, c], 16) for c in range(3)
        ]
        trace.append((picked[0] + picked[1] + picked[2]) / 3.0)
    out[0, 0] = motion[...]
    out[0, 1] = trace[1]
    out[0, 2] = trace[0]
    out[0, 3] = engaged[...].astype(jnp.float32) * factor[...]
    out[0, 4] = gaps[2] + nitsche * (gaps[0] - gaps[1])
    corners_out[...] = corners[...]


def element_total(field, vertices, entries, total, coarse_at, fine_at, body=0, chunks=range(8)):
    highs = keys(32, True)
    lows = keys(LOW)
    order = ((0, 4, 5, 6), (4, 1, 7, 8), (5, 7, 2, 9), (6, 8, 9, 3))
    for j in chunks:
        here = slice(ROWS * j, ROWS * (j + 1))
        corner = [vertices[body, pl.ds(32 * j + c, ROWS, stride=4), :] for c in range(4)]
        picked = [lane_lookup(lambda r: wide(field, r, body), i, 16) for i in corner]
        k = [entries[body, e, here, :] for e in range(10)]
        for c in range(4):
            o = order[c]
            row = (
                k[o[0]] * picked[0]
                + k[o[1]] * picked[1]
                + k[o[2]] * picked[2]
                + k[o[3]] * picked[3]
            )
            coarse, fine = split(row)
            coarse_at[body, c, here] = coarse
            fine_at[body, c, here] = fine
        slices = [
            scatter_operands(
                wide(vertices, 32 * j + 4 * s + c, body),
                wide(coarse_at, ROWS * j + s, body, c),
                wide(fine_at, ROWS * j + s, body, c),
                highs,
                lows,
            )
            for c in range(4)
            for s in range(ROWS)
        ]
        total = total + contract(slices)
    return total


def nothing():
    return jnp.zeros((64, LOW), jnp.float32)


def disc_kernel(field, vertices, entries, partners, out, lookup, coarse_at, fine_at):
    for g in range(4):
        for s in range(ROWS):
            lookup[pl.ds(64 * g + s, ROWS, stride=ROWS), :] = partners[
                ROWS * g : ROWS * (g + 1), LANES * s : LANES * (s + 1)
            ]
    out[...] = element_total(
        field, vertices, entries, nothing(), coarse_at, fine_at, chunks=range(DISC_FIRST)
    )


def middle_kernel(
    field, vertices, entries, pad_field, pad_vertices, pad_entries, disc, disc_out, pad_out, coarse_at, fine_at
):
    disc_out[...] = element_total(
        field, vertices, entries, disc[...], coarse_at.at[0], fine_at.at[0], chunks=range(2)
    )
    pad_out[...] = element_total(
        pad_field, pad_vertices, pad_entries, nothing(), coarse_at.at[1], fine_at.at[1], chunks=range(4)
    )


def rim_lookup(first_row, second_row, index):
    first = lane_lookup(first_row, index, 16)
    second = lane_lookup(second_row, index, 16)
    place = lax.broadcasted_iota(jnp.int32, (ROWS, LANES), 0)
    return jnp.where(place < 4, first, second)


def rim_slots(rims, slot_out):
    highs = keys(32, True)
    lows = keys(LOW)
    lane = lax.broadcasted_iota(jnp.int32, (ROWS, LANES), 1)
    for body in range(2):
        slices = []
        for s in range(4):
            coarse, fine = split((lane + (LANES * s + 1)).astype(jnp.float32))
            slices.append(scatter_operands(wide(rims, 4 * body + s), coarse, fine, highs, lows))
        store_nodal(slot_out, (body,), contract(slices))


def pad_kernel(
    field, vertices, entries, rims, whole, storage, disc, pad,
    out, rim_out, rims_out, slot_out, field_out, storage_out, coarse_at, fine_at,
):
    rims_out[...] = rims[...]
    field_out[...] = whole[...]
    storage_out[...] = storage[...]
    rim_slots(rims, slot_out)
    store_nodal(out, (0,), disc[...], -1.0)
    total = element_total(
        field, vertices, entries, pad[...], coarse_at, fine_at, chunks=range(4)
    )
    store_nodal(out, (1,), total, -1.0)
    rim_out[...] = rim_lookup(lambda r: wide(out, r, 0), lambda r: wide(out, r, 1), rims[...])


def source_of(face, place):
    z = (face >> 2) + AHEAD[place % 8]
    near = (face & 3) ^ ((2 if place & 8 else 0) | (1 if place & 16 else 0))
    return ((z & 7) << 2) | near


def packet_work(face, packets, own, lookup, normal, trace, total, coarse_at, fine_at):
    highs = keys(16, True)
    lows = keys(LOW)
    mine = lookup[pl.ds(pl.multiple_of(face * ROWS, ROWS), ROWS), :]
    n = 0
    for ref, first, count in packets:
        for group in range(0, count, 4):
            slices = []
            for at in range(group, min(group + 4, count)):
                source = source_of(face, first + at)
                chosen = (mine >> 10) == source
                local = mine & 1023
                normal = jnp.where(chosen, lane_lookup(lambda r: wide(ref, r, at, 0), local, 8), normal)
                trace = jnp.where(chosen, lane_lookup(lambda r: wide(ref, r, at, 1), local, 8), trace)

                index = lookup[pl.ds(pl.multiple_of(source * ROWS, ROWS), ROWS), :]
                local = index & 1023
                pad_normal = lane_lookup(lambda r: wide(own, r, 0, 0), local, 8)
                pad_trace = lane_lookup(lambda r: wide(own, r, 0, 1), local, 8)
                rate = (
                    ref[at, 3]
                    * (film_floor + jnp.maximum(ref[at, 4] - nitsche * pad_normal, 0.0))
                    * (pad_trace - ref[at, 2])
                )
                coarse, fine = split(jnp.where((index >> 10) == face, rate, 0.0))
                coarse_at[n] = coarse
                fine_at[n] = fine
                slices += [
                    scatter_operands(
                        wide(lookup, source * ROWS + s) & 1023,
                        wide(coarse_at, s, n),
                        wide(fine_at, s, n),
                        highs,
                        lows,
                    )
                    for s in range(ROWS)
                ]
                n += 1
            total = total + contract(slices)
    return normal, trace, total


def first_kernel(eight, twin, three, lookup, own, normal_out, trace_out, total_out, coarse_at, fine_at):
    zero = jnp.zeros((ROWS, LANES), jnp.float32)
    normal_out[...], trace_out[...], total_out[...] = packet_work(
        lax.axis_index("face"), ((eight, 0, 8), (twin, 16, 8), (three, 8, 3)), own, lookup,
        zero, zero, jnp.zeros((32, LOW), jnp.float32), coarse_at, fine_at,
    )


def second_kernel(
    three, five, lookup, own, normal, trace, total, normal_out, trace_out, total_out, coarse_at, fine_at
):
    normal_out[...], trace_out[...], total_out[...] = packet_work(
        lax.axis_index("face"), ((three, 24, 3), (five, 11, 5)), own, lookup,
        normal[...], trace[...], total[...], coarse_at, fine_at,
    )


def contact_kernel(
    last, lookup, own, normal, trace, total, corners, rims, element,
    pressure_out, nodal, rim_out, pads, coarse_at, fine_at,
):
    pad_normal, pad_trace, total = packet_work(
        lax.axis_index("face"), ((last, 27, 5),), own, lookup,
        normal[...], trace[...], total[...], coarse_at, fine_at,
    )
    weight = own[0, 3]
    pressure = jnp.where(
        weight != 0.0, jnp.maximum(own[0, 4] - nitsche * pad_normal, 0.0), 0.0
    )
    pressure_out[...] = pressure
    disc_rate = weight * (film_floor + pressure) * (pad_trace - own[0, 2])
    store_nodal(pads, (), total, -1.0)

    highs = keys(32, True)
    lows = keys(LOW)
    for body in range(2):
        rate = disc_rate if body == 0 else pads[...]
        coarse, fine = split(rate / 3.0)
        at = 8 + body
        coarse_at[at] = coarse
        fine_at[at] = fine
        slices = [
            scatter_operands(
                wide(corners, s, body, c), wide(coarse_at, s, at), wide(fine_at, s, at), highs, lows
            )
            for c in range(3)
            for s in range(ROWS)
        ]
        store_nodal(nodal, (body,), contract(slices))
        nodal[body] = nodal[body] + element[body]
    rim_out[...] = rim_lookup(lambda r: wide(nodal, r, 0), lambda r: wide(nodal, r, 1), rims[...])


def inner_kernel(
    field, vertices, entries, rims, storage, partners, engaged, gaps, motion,
    out, rim_out, slot_out, field_out, storage_out, mine, active, gaps_out, normals, coarse_at, fine_at,
):
    field_out[...] = field[...]
    storage_out[...] = storage[...]
    active[...] = engaged[...].astype(jnp.float32)
    gaps_out[...] = gaps[...]
    for patch in range(32):
        normals[patch] = motion[...]
    face = lax.axis_index("face")
    place = lax.broadcasted_iota(jnp.int32, (ROWS, LANES), 0)
    faces = jnp.zeros((ROWS, LANES), jnp.int32)
    for s in range(ROWS):
        block = partners[
            pl.ds(pl.multiple_of(face & -ROWS, ROWS), ROWS), LANES * s : LANES * (s + 1)
        ]
        row = jnp.sum(jnp.where(place == (face & (ROWS - 1)), block, 0), axis=0, keepdims=True)
        faces = jnp.where(place == s, row, faces)
    mine[...] = faces
    rim_slots(rims, slot_out)
    for body in range(2):
        total = element_total(field, vertices, entries, nothing(), coarse_at, fine_at, body)
        store_nodal(out, (body,), total, -1.0)
    rim_out[...] = rim_lookup(lambda r: wide(out, r, 0), lambda r: wide(out, r, 1), rims[...])


def pressure_kernel(normals, mine, active, gaps, out):
    patch = mine[...] >> 10
    local = mine[...] & 1023
    normal = jnp.zeros((ROWS, LANES), jnp.float32)
    for source in range(32):
        found = lane_lookup(lambda r: wide(normals, r, source), local, 8)
        normal = jnp.where(patch == source, found, normal)
    out[...] = active[...] * jnp.maximum(gaps[2] + nitsche * (gaps[0] - normal - gaps[1]), 0.0)


def advance_kernel(field, storage, nodal, slots, early, late, out, gained):
    place = lax.broadcasted_iota(jnp.int32, (ROWS, LANES), 0)
    depth = lax.axis_index("depth")
    even = (depth & 1) == 0
    other = jnp.where((depth > 0) & (depth < 7), early[...], 0.0)
    above = jnp.where(even, late[...], other)
    below = jnp.where(even, other, late[...])
    gained[...] = jnp.where((place & 1) == 0, pltpu.roll(below, 7, 0), pltpu.roll(above, 1, 0))
    for body in range(2):
        for half in range(2):
            here = slice(ROWS * half, ROWS * (half + 1))
            slot = slots[body, here].astype(jnp.int32)
            found = lane_lookup(
                lambda r: wide(gained, 4 * body + r), jnp.maximum(slot - 1, 0), 4
            )
            total = nodal[body, here] + jnp.where(slot > 0, found, 0.0)
            out[body, here] = field[body, here] + increment_factor * total / storage[body, here]


def here(*shape, dtype=jnp.float32):
    return pltpu.VMEM(shape, dtype)


class Placed:
    def __init__(self, array, near):
        self.array, self.near = array, near

    @staticmethod
    def of(argument):
        return argument if isinstance(argument, Placed) else Placed(argument, False)


def near(array):
    return Placed(array, True)


def one_body(array, body, part=0, parts=1):
    block = (1,) + array.shape[1:-2] + (array.shape[-2] // parts, LANES)
    at = (body,) + (0,) * (len(block) - 3) + (part, 0)
    return pl.BlockSpec(block, lambda i: at, memory_space=pltpu.VMEM)


def call(body, out, arguments, scratch=(), specs=None, name=None, time=1.0):
    whole = pl.BlockSpec(memory_space=pltpu.VMEM)
    specs = specs or {}
    arguments = tuple(
        pltpu.with_memory_space_constraint(a.array, pltpu.VMEM if a.near else pltpu.HBM)
        for a in map(Placed.of, arguments)
    )
    return pl.pallas_call(
        body,
        out_shape=out,
        in_specs=[specs.get(i, whole) for i in range(len(arguments))],
        out_specs=jax.tree.map(lambda _: whole, out),
        scratch_shapes=[pltpu.VMEM(s, jnp.float32) for s in scratch],
        grid=(1,) if specs else (),
        name=name,
        cost_estimate=pl.CostEstimate(
            flops=0, transcendentals=0, bytes_accessed=int(time * 3.6e6)
        ),
    )(*arguments)


def local(
    thermal_field,
    lumped_storage,
    simplex_vertices,
    stiffness_entries,
    interface_vertices,
    touching_triangle_vertices,
    partner_lookup,
    engaged_flags,
    rotor_gap_quantities,
    lining_orthogonal_motion,
    touching_transfer_factor,
):
    field = thermal_field.reshape(2, 16, LANES)
    storage = lumped_storage.reshape(2, 16, LANES)
    vertices = simplex_vertices.reshape(2, 4, 64, LANES).transpose(0, 2, 1, 3).reshape(2, 256, LANES)
    entries = stiffness_entries.reshape(2, 10, 64, LANES)
    rims = interface_vertices.reshape(2, 2, 2, LANES).transpose(0, 2, 1, 3).reshape(8, LANES)
    corners = touching_triangle_vertices.reshape(2, 3, ROWS, LANES)
    engaged = engaged_flags.reshape(ROWS, LANES)
    gaps = rotor_gap_quantities.reshape(3, ROWS, LANES)
    motion = lining_orthogonal_motion.reshape(ROWS, LANES)
    factor = touching_transfer_factor.reshape(ROWS, LANES)
    tile = here(ROWS, LANES)
    nodes = here(16, LANES)
    sums = (tile, tile, here(32, LOW))

    def along(cells, step):
        return lax.ppermute(cells, "face", [(i, (i + 4 * step) % 32) for i in range(32)])

    def across(cells, bit):
        return lax.ppermute(cells, "face", [(i, i ^ bit) for i in range(32)])

    def of_body(body, part=0, parts=1):
        return (one_body(field, body), one_body(vertices, body, part, parts), one_body(entries, body, part, parts))

    bodies = (field, vertices, entries)
    partial = here(64, LOW)

    def elements_and_eight(own):
        behind = along(own, 1)
        ahead = along(own, -1)
        disc, lookup = call(
            disc_kernel,
            (partial, here(256, LANES, dtype=jnp.int32)),
            (*bodies, partner_lookup),
            scratch=((1, 4, 64, LANES),) * 2,
            specs=dict(enumerate(of_body(0))),
            name="disc_element",
            time=2.2,
        )
        behind, ahead, disc, lookup = lax.optimization_barrier((behind, ahead, disc, lookup))
        three = jnp.concatenate([behind, own, ahead], axis=0)
        three, again = lax.optimization_barrier((three, field))
        far_ahead = along(three, -3)
        far_behind = along(three[:2], 2)
        other_three = across(three, 2)
        disc, pad = call(
            middle_kernel,
            (partial, partial),
            (again, vertices, entries, *bodies, near(disc)),
            scratch=((2, 1, 4, 32, LANES),) * 2,
            specs=dict(enumerate(of_body(0, 3, 4) + of_body(1, 0, 2))),
            name="middle_element",
            time=2.2,
        )
        far_ahead, far_behind, disc, pad = lax.optimization_barrier(
            (far_ahead, far_behind, disc, pad)
        )
        five = jnp.concatenate([far_ahead, far_behind], axis=0)
        eight = jnp.concatenate([three, five], axis=0)
        return eight, five, other_three, lookup, disc, pad

    def surface_block():
        own, own_corners = call(
            packet_kernel,
            (here(1, 5, ROWS, LANES), here(2, 3, ROWS, LANES, dtype=jnp.int32)),
            (field, corners, motion, engaged, gaps, factor),
            name="packet",
        )
        eight, five, other_three, lookup, disc, pad = elements_and_eight(own)
        other_five = across(five, 2)
        twin = across(eight, 1)
        last_three = across(other_three, 1)
        done = call(
            first_kernel,
            sums,
            (near(eight), near(twin), near(other_three), near(lookup), near(own)),
            scratch=((19, ROWS, LANES),) * 2,
            name="first_packets",
            time=1.5,
        )
        again, disc, done = lax.optimization_barrier((field, disc, done))
        element, rim_element, rims_near, *kept = call(
            pad_kernel,
            (here(2, 16, LANES), tile, here(ROWS, LANES, dtype=jnp.int32))
            + (here(2, 16, LANES),) * 3,
            (again, vertices, entries, rims, field, storage, near(disc), near(pad)),
            scratch=((1, 4, 32, LANES),) * 2,
            specs=dict(enumerate(of_body(1, 1, 2))),
            name="pad_element",
            time=2.2,
        )
        other_five, last_three, done, element = lax.optimization_barrier(
            (other_five, last_three, done, element)
        )
        last = across(other_five, 1)
        done = call(
            second_kernel,
            sums,
            (near(last_three), near(other_five), near(lookup), near(own), *map(near, done)),
            scratch=((8, ROWS, LANES),) * 2,
            name="second_packets",
        )
        last, done = lax.optimization_barrier((last, done))
        pressure, nodal, rim_total = call(
            contact_kernel,
            (tile, here(2, 16, LANES), tile),
            tuple(map(near, (last, lookup, own, *done, own_corners, rims_near, element))),
            scratch=((ROWS, LANES), (10, ROWS, LANES), (10, ROWS, LANES)),
            name="contact",
            time=1.5,
        )
        return pressure, nodal, rim_total, rim_element, *kept

    def inner_block():
        element, rim_element, *kept, mine, active, gaps_near, normals = call(
            inner_kernel,
            (here(2, 16, LANES), tile)
            + (here(2, 16, LANES),) * 3
            + (here(ROWS, LANES, dtype=jnp.int32), tile, here(3, ROWS, LANES), here(32, ROWS, LANES)),
            (field, vertices, entries, rims, storage, partner_lookup, engaged, gaps, motion),
            scratch=((2, 4, 64, LANES),) * 2,
            name="inner_elements",
            time=4.5,
        )
        early = lax.ppermute(rim_element, "depth", [(1, 2), (2, 1), (3, 4), (4, 3), (5, 6), (6, 5)])
        normals = lax.all_to_all(normals, "face", 0, 0, tiled=True)
        pressure = call(
            pressure_kernel,
            tile,
            tuple(map(near, (normals, mine, active, gaps_near))),
            name="pressure",
        )
        return pressure, element, rim_element, early, *kept

    pressure, nodal, rim_total, early, slots, field_near, storage_near = lax.cond(
        lax.axis_index("depth") == 0, surface_block, inner_block
    )
    late = lax.ppermute(rim_total, "depth", [(i, i ^ 1) for i in range(8)])
    advanced = call(
        advance_kernel,
        jax.ShapeDtypeStruct((2, 16, LANES), jnp.float32),
        tuple(map(near, (field_near, storage_near, nodal, slots, early, late))),
        scratch=((ROWS, LANES),),
        name="advance",
    )
    return advanced.reshape(thermal_field.shape), pressure.reshape(1, 1024)


def solution(mesh):
    placed = (
        P(None, "face", "depth", None),
        P(None, "face", "depth", None),
        P(None, "face", "depth", None, None),
        P(None, "face", "depth", None, None),
        P(None, "face", "depth", None, None),
        P(None, "face", None, None),
        P(),
        P("face", None),
        P(None, "face", None),
        P("face", None),
        P("face", None),
    )
    return jax.shard_map(
        local,
        mesh=mesh,
        in_specs=placed,
        out_specs=(P(None, "face", "depth", None), P("face", None)),
        check_vma=False,
    )
```
